512 devices in a mesh: ctx: 64 (over z, y), head: 8 (over x, core).
Axes of the slice: x: 4, y: 4, z: 16, core: 2. Of those that a mesh axis runs over, the one named last changes fastest.
Arguments:
- queries: bfloat16 [16384, 4096], P('ctx', 'head'), may hold values from -6 to 6
- keys: bfloat16 [16384, 4096], P('ctx', 'head'), may hold values from -6 to 6
- values: bfloat16 [16384, 4096], P('ctx', 'head'), may hold values from -70 to 70
- d_out: bfloat16 [16384, 4096], P('ctx', 'head'), may hold values from -6 to 6
- gain: float32 [4096], P('head'), may hold values from 0.25 to 1.75
- live_rows: int32 [64], P('ctx'), may hold values from 64 to 256, as said below
- doc_start: int32 [16384], P('ctx'), may hold values from 0 to 1, as said below
Outputs:
- normed: bfloat16 [16384, 4096], P('ctx', 'head')
- grad_queries: bfloat16 [16384, 4096], P('ctx', 'head')
- grad_keys: bfloat16 [16384, 4096], P('ctx', 'head')
- grad_values: bfloat16 [16384, 4096], P('ctx', 'head')
- grad_gain: float32 [4096], P('head')
The draws below stay inside these ranges and needn't reach their ends.
Inputs may be any that keep to these rules, and one draw needn't show every extreme that they name: `live_rows`: some block is full in every draw. `doc_start`: flags on rows that are not live are ignored.
All inputs are finite; a program needn't handle non-finite values.
Results may differ from the reference program's by a relative error of at most 0.0052.
Values sent between devices are 32-bit elements; how exact they have to be, the bound alone decides.
A program may use at most 64 MiB of HBM per device.

```python
import jax
import jax.numpy as jnp
from jax import lax

HEADS = 32
HEAD_DIM = 128
TOK_DEV = 256
D = 4096
SHARDS = 64
ROWS = 16384


def draw_values(key, part):
    first, second, third = jax.random.split(key, 3)
    head_of = (jnp.arange(D) // HEAD_DIM).astype(jnp.float32)
    steps = float(max(HEADS - 1, 1))
    base = jnp.clip(jax.random.normal(first, (ROWS, D), jnp.float32), -4.0, 4.0)
    trend = 3.0 ** (0.5 * head_of / steps)
    column_scale = 10.0 ** jax.random.uniform(second, (D,), jnp.float32, -0.5, 0.5)
    row_scale = 10.0 ** jax.random.uniform(third, (ROWS, 1), jnp.float32, -0.5, 0.5)
    return (base * trend[None, :] * column_scale[None, :] * row_scale).astype(jnp.bfloat16)


def draw_live_rows(key, part):
    counts = jax.random.randint(key, (SHARDS,), TOK_DEV // 4, TOK_DEV + 1)
    forced = jax.random.randint(jax.random.fold_in(key, 7), (), 0, SHARDS)
    return jnp.where(jnp.arange(SHARDS) == forced, TOK_DEV, counts).astype(jnp.int32)


def draw_doc_start(key, part):
    start_draw = jax.random.randint(key, (ROWS,), 0, 8 * TOK_DEV) == 0
    forced = jax.random.randint(jax.random.fold_in(key, 11), (), 0, ROWS)
    return jnp.where(jnp.arange(ROWS) == forced, True, start_draw).astype(jnp.int32)


def shard_levels(key, dims, cuts, low, top_value):
    def one(dim, parts):
        steps = jax.random.uniform(jax.random.fold_in(jax.random.fold_in(key, 6), dim), (parts,), jnp.float32, low / len(cuts), top_value / len(cuts))
        return jnp.repeat(jnp.exp(steps), dims[dim] // parts).reshape((-1,) + (1,) * (len(dims) - dim - 1))

    loudness = one(*cuts[0])
    for cut in cuts[1:]:
        loudness = loudness * one(*cut)
    return loudness


def normal_values(stream_key, shape, scale, limit, cuts=(), kind=jnp.bfloat16):
    drawn = scale * jax.random.normal(stream_key, shape, jnp.float32)
    if cuts:
        drawn = drawn * shard_levels(stream_key, shape, cuts, -0.22, 0.18)
    return jnp.clip(drawn, -limit, limit).astype(kind)


def setup_inputs(seed: int = 0) -> dict:
    splits = jax.random.split(jax.random.key(seed), 8)
    queries = normal_values(splits[0], (ROWS, D), 1.0, 6.0, ((0, 64), (1, 8)))
    keys = normal_values(splits[1], (ROWS, D), 1.0, 6.0, ((0, 64), (1, 8)))
    values = draw_values(jax.random.fold_in(splits[7], 71), 0)
    d_out = normal_values(splits[3], (ROWS, D), 1.0, 6.0, ((0, 64), (1, 8)))
    gain = jnp.clip(1.0 + 0.15 * jax.random.normal(splits[4], (D,), jnp.float32), 0.25, 1.75)
    live_rows = draw_live_rows(jax.random.fold_in(splits[7], 71), 0)
    doc_start = draw_doc_start(jax.random.fold_in(splits[7], 71), 0)
    return dict(queries=queries, keys=keys, values=values, d_out=d_out, gain=gain, live_rows=live_rows, doc_start=doc_start)


epsilon = 1e-06

def pair_mask(live_mask, doc_ids):
    count = doc_ids.shape[0]
    position = jnp.arange(count, dtype=jnp.int32)
    order_ok = position[None, :] <= position[:, None]
    return (doc_ids[:, None] == doc_ids[None, :]) & order_ok & live_mask[:, None] & live_mask[None, :]

def weights_of(query_block, key_block, live_mask, doc_ids):
    scores = jnp.einsum('thf,shf->hts', query_block.astype(jnp.float32), key_block.astype(jnp.float32))
    return jnp.where(pair_mask(live_mask, doc_ids)[None], scores, 0.0).astype(jnp.bfloat16)

def reference(queries, keys, values, d_out, gain, live_rows, doc_start):
    row_count = queries.shape[0]
    model_width = queries.shape[1]
    row_index = jnp.arange(row_count, dtype=jnp.int32)
    live_mask = row_index % TOK_DEV < live_rows[row_index // TOK_DEV]
    start_flags = jnp.where(live_mask, doc_start, 0).astype(jnp.int32)
    doc_ids = jnp.cumsum(start_flags).astype(jnp.int32)
    before_ids = (doc_ids - start_flags).astype(jnp.int32)

    def blocked(array):
        return array.reshape(SHARDS, TOK_DEV, HEADS, HEAD_DIM)
    query_blocks = blocked(queries)
    key_blocks = blocked(keys)
    value_blocks = blocked(values)
    live_blocks = live_mask.reshape(SHARDS, TOK_DEV)
    doc_blocks = doc_ids.reshape(SHARDS, TOK_DEV)
    before_blocks = before_ids.reshape(SHARDS, TOK_DEV)
    zero_state = jnp.zeros((HEADS, HEAD_DIM, HEAD_DIM), jnp.float32)
    no_doc = jnp.array(-1, jnp.int32)
    highest = lax.Precision.HIGHEST

    def forward(carry, inputs):
        state, carry_doc = carry
        query_block, key_block, value_block, live_block, doc_block = inputs
        weights = weights_of(query_block, key_block, live_block, doc_block)
        local_part = jnp.einsum('hts,shf->thf', weights.astype(jnp.float32), value_block.astype(jnp.float32))
        take = (live_block & (doc_block == carry_doc)).astype(jnp.float32)[:, None, None]
        carried = jnp.einsum('thf,hfg->thg', query_block.astype(jnp.float32), state, precision=highest) * take
        last_doc = doc_block[-1]
        keep = (live_block & (doc_block == last_doc))[:, None, None]
        tail_keys = jnp.where(keep, key_block, jnp.zeros_like(key_block)).astype(jnp.float32)
        tail_state = jnp.einsum('thf,thg->hfg', tail_keys, value_block.astype(jnp.float32))
        new_state = state * (last_doc == carry_doc).astype(jnp.float32) + tail_state
        return ((new_state, last_doc), local_part + carried)
    _, attended = lax.scan(forward, (zero_state, no_doc), (query_blocks, key_blocks, value_blocks, live_blocks, doc_blocks))
    attended = attended.reshape(row_count, model_width)
    upstream = d_out.astype(jnp.float32)
    scaled = gain[None, :] * upstream
    square_sum = lax.optimization_barrier(jnp.sum(attended * attended, axis=1))
    inner_sum = lax.optimization_barrier(jnp.sum(scaled * attended, axis=1))
    radius = jnp.sqrt(square_sum / model_width + epsilon)
    normed = (attended / radius[:, None] * gain[None, :]).astype(jnp.bfloat16)
    grad_att = scaled / radius[:, None] - attended * (inner_sum / (model_width * radius ** 3))[:, None]
    grad_att = jnp.where(live_mask[:, None], grad_att, 0.0).astype(jnp.bfloat16)
    grad_gain = lax.optimization_barrier(jnp.sum(upstream * attended / radius[:, None], axis=0))
    grad_blocks = blocked(grad_att)

    def probe_of(grad_block, value_block, live_block, doc_block):
        probe_scores = jnp.einsum('thg,shg->hts', grad_block.astype(jnp.float32), value_block.astype(jnp.float32))
        return jnp.where(pair_mask(live_block, doc_block)[None], probe_scores, 0.0).astype(jnp.bfloat16)

    def query_pass(carry, inputs):
        state, carry_doc = carry
        query_block, key_block, value_block, grad_block, live_block, doc_block = inputs
        probe_weights = probe_of(grad_block, value_block, live_block, doc_block)
        take = (live_block & (doc_block == carry_doc)).astype(jnp.float32)[:, None, None]
        grad_query = jnp.einsum('hts,shf->thf', probe_weights.astype(jnp.float32), key_block.astype(jnp.float32))
        grad_query = grad_query + jnp.einsum('thg,hfg->thf', grad_block.astype(jnp.float32), state, precision=highest) * take
        last_doc = doc_block[-1]
        keep = (live_block & (doc_block == last_doc))[:, None, None]
        tail_keys = jnp.where(keep, key_block, jnp.zeros_like(key_block)).astype(jnp.float32)
        tail_state = jnp.einsum('thf,thg->hfg', tail_keys, value_block.astype(jnp.float32))
        new_state = state * (last_doc == carry_doc).astype(jnp.float32) + tail_state
        return ((new_state, last_doc), grad_query)
    _, grad_queries = lax.scan(query_pass, (zero_state, no_doc), (query_blocks, key_blocks, value_blocks, grad_blocks, live_blocks, doc_blocks))

    def key_pass(carry, inputs):
        state, carry_doc = carry
        query_block, key_block, value_block, grad_block, live_block, doc_block, before_block = inputs
        weights = weights_of(query_block, key_block, live_block, doc_block)
        probe_weights = probe_of(grad_block, value_block, live_block, doc_block)
        take = (live_block & (doc_block == carry_doc)).astype(jnp.float32)[:, None, None]
        grad_key = jnp.einsum('hts,thf->shf', probe_weights.astype(jnp.float32), query_block.astype(jnp.float32))
        grad_key = grad_key + jnp.einsum('shg,hfg->shf', value_block.astype(jnp.float32), state, precision=highest) * take
        grad_value = jnp.einsum('hts,thg->shg', weights.astype(jnp.float32), grad_block.astype(jnp.float32))
        grad_value = grad_value + jnp.einsum('shf,hfg->shg', key_block.astype(jnp.float32), state, precision=highest) * take
        head_doc = before_block[0]
        keep = (live_block & (doc_block == head_doc))[:, None, None]
        head_queries = jnp.where(keep, query_block, jnp.zeros_like(query_block)).astype(jnp.float32)
        head_state = jnp.einsum('thf,thg->hfg', head_queries, grad_block.astype(jnp.float32))
        new_state = state * (doc_block[-1] == head_doc).astype(jnp.float32) + head_state
        return ((new_state, head_doc), (grad_key, grad_value))
    _, (grad_keys, grad_values) = lax.scan(key_pass, (zero_state, no_doc), (query_blocks, key_blocks, value_blocks, grad_blocks, live_blocks, doc_blocks, before_blocks), reverse=True)
    return (normed, grad_queries.reshape(row_count, model_width).astype(jnp.bfloat16), grad_keys.reshape(row_count, model_width).astype(jnp.bfloat16), grad_values.reshape(row_count, model_width).astype(jnp.bfloat16), grad_gain)
```

```python
import jax
import jax.numpy as jnp
from jax import lax
from jax.experimental import pallas as pl
from jax.experimental.pallas import tpu as pltpu
from jax.sharding import PartitionSpec as P

HEADS = 32
HEAD_DIM = 128
D = HEADS * HEAD_DIM
EPSILON = 1e-06
ROWS = 256
LOCAL = 4
CUBE = 16
GROUPS = 4
PIECE = 32
HEAD_PEERS = 8
MESH = pl.DeviceIdType.MESH
F32 = jnp.float32
BF16 = jnp.bfloat16


def dot(a, b, ca, cb):
    return lax.dot_general(a, b, (((ca,), (cb,)), ((), ())), preferred_element_type=F32)


def halves(x):
    upper = x.astype(BF16)
    return upper, (x - upper.astype(F32)).astype(BF16)


def kernel(
    q_hbm, k_hbm, v_hbm, y_hbm, gain_ref, live_ref, doc_ref,
    normed_hbm, dq_hbm, dk_hbm, dv_hbm, dgain_ref,
    q_ref, k_ref, v_ref, y_ref,
    mask_ref, w_ref, att_ref, ga_ref, gh_ref, qh_ref, qht_ref, kt_ref, vt_ref,
    normed_ref, dq_ref, dk_ref, dv_ref, dkl_ref, dvl_ref,
    flag_src, flag_buf, keep_buf,
    t_ref, tin_ref, pre_ref, tot_ref, totin_ref, carry_ref, sout_ref, s_ref,
    h_ref, hin_ref, suf_ref, htot_ref, htotin_ref, rout_ref, r_ref,
    ps_src, ps_buf, gg_src, gg_buf, gt_src, gt_buf,
    in_sem, out_sem,
    fs, fr, l1s, l1r, l2s, l2r, l3s, l3r, pss, psr,
    b1s, b1r, b2s, b2r, b3s, b3r, g1s, g1r, g2s, g2r,
):
    c = lax.axis_index("ctx")
    me = lax.axis_index("head")
    p = lax.rem(c, CUBE)
    g = lax.div(c, CUBE)
    base = g * CUBE

    def rank(a):
        return lax.rem(p + a, CUBE)

    barrier = pltpu.get_barrier_semaphore()
    for a in range(1, CUBE):
        pl.semaphore_signal(barrier, inc=1, device_id={"ctx": base + rank(a)}, device_id_type=MESH)
    for b in range(1, GROUPS):
        pl.semaphore_signal(
            barrier, inc=1, device_id={"ctx": lax.rem(g + b, GROUPS) * CUBE + p}, device_id_type=MESH
        )
    for a in range(1, HEAD_PEERS):
        pl.semaphore_signal(
            barrier, inc=1, device_id={"head": lax.rem(me + a, HEAD_PEERS)}, device_id_type=MESH
        )

    loads = [
        pltpu.make_async_copy(src, dst, in_sem.at[i])
        for i, (src, dst) in enumerate(
            ((k_hbm, k_ref), (v_hbm, v_ref), (q_hbm, q_ref), (y_hbm, y_ref))
        )
    ]
    for load in loads:
        load.start()

    def remote(src, dst, send, recv, where):
        return pltpu.make_async_remote_copy(
            src_ref=src, dst_ref=dst, send_sem=send, recv_sem=recv, device_id=where, device_id_type=MESH
        )

    live = live_ref[0]
    lane = lax.broadcasted_iota(jnp.int32, (ROWS, ROWS), 1)
    sub = lax.broadcasted_iota(jnp.int32, (ROWS, ROWS), 0)
    row8 = lax.broadcasted_iota(jnp.int32, (8, ROWS), 1)
    docs = jnp.broadcast_to(doc_ref[...].reshape(1, ROWS), (8, ROWS))
    starts = jnp.where(row8 < live, docs, 0).astype(F32).astype(BF16)
    upto = jnp.where(sub <= lane, 1.0, 0.0).astype(BF16)
    since = jnp.where(lane <= sub, 1.0, 0.0).astype(BF16)
    id_row = dot(starts, upto, 1, 0)[0:1, :]
    id_col = dot(since, starts, 1, 1)[:, 0:1]
    last = id_row[:, ROWS - 1 : ROWS]
    col = lax.broadcasted_iota(jnp.int32, (ROWS, 1), 0)
    live_col = jnp.where(col < live, 1.0, 0.0)
    tail_col = jnp.where(id_col == last, live_col, 0.0)
    head_col = jnp.where(id_col == 0.0, live_col, 0.0)
    flag = jnp.broadcast_to(jnp.where(last > 0.0, 1.0, 0.0), (1, HEAD_DIM))
    flag_src[...] = flag
    flag_buf[p] = flag
    mask_ref[...] = jnp.where((id_col == id_row) & (lane <= sub), live_col, 0.0)
    tail_b = jnp.broadcast_to(tail_col, (ROWS, HEAD_DIM)).astype(BF16)
    head_b = jnp.broadcast_to(head_col, (ROWS, HEAD_DIM)).astype(BF16)
    live_b = jnp.broadcast_to(live_col, (ROWS, HEAD_DIM))

    def cols(h):
        return pl.ds(h * HEAD_DIM, HEAD_DIM)

    loads[0].wait()
    loads[1].wait()
    for h in range(LOCAL):
        kt = k_ref[:, cols(h)] * tail_b
        kt_ref[:, cols(h)] = kt
        t_ref[pl.ds(4 * h, 4)] = dot(kt, v_ref[:, cols(h)], 0, 0).reshape(4, PIECE, HEAD_DIM)
    tin_ref[p] = t_ref[p]

    pl.semaphore_wait(barrier, CUBE - 1 + GROUPS - 1 + HEAD_PEERS - 1)

    flags = [
        remote(flag_src, flag_buf.at[p], fs.at[a], fr.at[a], {"ctx": base + rank(a)}) for a in range(1, CUBE)
    ]
    level1 = [
        remote(t_ref.at[rank(a)], tin_ref.at[p], l1s.at[a], l1r.at[a], {"ctx": base + rank(a)})
        for a in range(1, CUBE)
    ]
    for copy in flags + level1:
        copy.start()

    loads[2].wait()
    for h in range(LOCAL):
        qs = q_ref[:, cols(h)]
        scores = dot(qs, k_ref[:, cols(h)], 1, 1)
        weights = (scores * mask_ref[...]).astype(BF16)
        w_ref[h] = weights
        att_ref[:, cols(h)] = dot(weights, v_ref[:, cols(h)], 1, 0)
        qh = qs * head_b
        qh_ref[:, cols(h)] = qh
        qht_ref[h] = qh.T
        vt_ref[:, cols(h)] = v_ref[:, cols(h)] * tail_b
    loads[3].wait()

    for copy in flags + level1:
        copy.wait_recv()

    acc = jnp.zeros((PIECE, HEAD_DIM), F32)
    keep = jnp.ones((1, HEAD_DIM), F32)
    for i in range(CUBE):
        pre_ref[i] = acc
        keep_buf[i] = keep
        hold = 1.0 - flag_buf[i]
        acc = tin_ref[i] + hold * acc
        keep = keep * hold
    flag_tile = jnp.broadcast_to(1.0 - keep, (8, HEAD_DIM))
    tot_ref[pl.ds(0, PIECE)] = acc
    tot_ref[pl.ds(PIECE, 8)] = flag_tile
    htot_ref[pl.ds(PIECE, 8)] = flag_tile

    def up(b):
        return remote(tot_ref, totin_ref.at[g], l2s.at[b], l2r.at[b], {"ctx": lax.rem(g + b, GROUPS) * CUBE + p})

    for b in range(1, GROUPS):
        @pl.when(g + b < GROUPS)
        def _():
            up(b).start()

    carry_ref[...] = jnp.zeros((PIECE, HEAD_DIM), F32)
    for b in range(GROUPS - 1, 0, -1):
        @pl.when(g - b >= 0)
        def _():
            up(b).wait_recv()
            at = lax.rem(g + GROUPS - b, GROUPS)
            hold = 1.0 - totin_ref[at, pl.ds(PIECE, 1), :]
            carry_ref[...] = totin_ref[at, pl.ds(0, PIECE), :] + hold * carry_ref[...]

    carry = carry_ref[...]
    level3 = []
    for a in range(1, CUBE):
        i = rank(a)
        sout_ref[i] = pre_ref[i] + keep_buf[i] * carry
        copy = remote(sout_ref.at[i], s_ref.at[p], l3s.at[a], l3r.at[a], {"ctx": base + i})
        copy.start()
        level3.append(copy)
    s_ref[p] = pre_ref[p] + keep_buf[p] * carry
    for copy in level3:
        copy.wait_recv()

    square = jnp.zeros((ROWS, HEAD_DIM), F32)
    inner = jnp.zeros((ROWS, HEAD_DIM), F32)
    for h in range(LOCAL):
        upper, lower = halves(s_ref[pl.ds(4 * h, 4)].reshape(HEAD_DIM, HEAD_DIM))
        qh = qh_ref[:, cols(h)]
        att = att_ref[:, cols(h)] + dot(
            jnp.concatenate([qh, qh], axis=1), jnp.concatenate([upper, lower], axis=0), 1, 0
        )
        att_ref[:, cols(h)] = att
        square = square + att * att
        inner = inner + att * (y_ref[:, cols(h)].astype(F32) * gain_ref[pl.ds(h * HEAD_DIM, HEAD_DIM)].reshape(1, HEAD_DIM))
    ones = jnp.ones((8, 2 * HEAD_DIM), BF16)
    sums = [dot(ones, jnp.concatenate(halves(x), axis=1), 1, 1)[0:1, :] for x in (square, inner)]
    sums = jnp.concatenate(sums, axis=1)
    ps_src[...] = sums
    ps_buf[me] = sums
    shared = [
        remote(ps_src, ps_buf.at[me], pss.at[a], psr.at[a], {"head": lax.rem(me + a, HEAD_PEERS)})
        for a in range(1, HEAD_PEERS)
    ]
    for copy in shared:
        copy.start()
    for copy in shared:
        copy.wait_recv()
    sums = ps_buf[0]
    for i in range(1, HEAD_PEERS):
        sums = sums + ps_buf[i]
    inverse = lax.rsqrt(sums[:, :ROWS] / D + EPSILON)
    factor = sums[:, ROWS:] * (inverse * inverse * inverse / D)
    inverse_col = jnp.broadcast_to(inverse, (HEAD_DIM, ROWS)).T
    factor_col = jnp.broadcast_to(factor, (HEAD_DIM, ROWS)).T

    back1 = []
    gain_terms = []
    for h in range(LOCAL):
        att = att_ref[:, cols(h)]
        y = y_ref[:, cols(h)].astype(F32)
        gains = gain_ref[pl.ds(h * HEAD_DIM, HEAD_DIM)].reshape(1, HEAD_DIM)
        ga = ((y * gains) * inverse_col - att * factor_col) * live_b
        ga = ga.astype(BF16)
        ga_ref[:, cols(h)] = ga
        h_ref[pl.ds(4 * h, 4)] = dot(qht_ref[h], ga, 1, 0).reshape(4, PIECE, HEAD_DIM)
    hin_ref[p] = h_ref[p]
    back1 = [
        remote(h_ref.at[rank(a)], hin_ref.at[p], b1s.at[a], b1r.at[a], {"ctx": base + rank(a)})
        for a in range(1, CUBE)
    ]
    for copy in back1:
        copy.start()

    for h in range(LOCAL):
        att = att_ref[:, cols(h)]
        y = y_ref[:, cols(h)].astype(F32)
        gains = gain_ref[pl.ds(h * HEAD_DIM, HEAD_DIM)].reshape(1, HEAD_DIM)
        unit = att * inverse_col
        normed_ref[:, cols(h)] = (unit * gains).astype(BF16)
        gain_terms.append(jnp.sum(y * unit, axis=0, keepdims=True))
    gain_term = jnp.concatenate(gain_terms, axis=1)
    gg_src[...] = gain_term
    gg_buf[p] = gain_term
    gain1 = [
        remote(gg_src, gg_buf.at[p], g1s.at[a], g1r.at[a], {"ctx": base + rank(a)}) for a in range(1, CUBE)
    ]
    for copy in gain1:
        copy.start()
    stores = [
        pltpu.make_async_copy(src, dst, out_sem.at[i])
        for i, (src, dst) in enumerate(
            ((normed_ref, normed_hbm), (dq_ref, dq_hbm), (dk_ref, dk_hbm), (dv_ref, dv_hbm))
        )
    ]
    stores[0].start()
    for h in range(LOCAL):
        ga = ga_ref[:, cols(h)]
        probes = (dot(ga, v_ref[:, cols(h)], 1, 1) * mask_ref[...]).astype(BF16)
        upper, lower = halves(s_ref[pl.ds(4 * h, 4)].reshape(HEAD_DIM, HEAD_DIM))
        gh = ga * head_b
        carried = dot(jnp.concatenate([gh, gh], axis=1), jnp.concatenate([upper, lower], axis=1), 1, 1)
        dq_ref[:, cols(h)] = (dot(probes, k_ref[:, cols(h)], 1, 0) + carried).astype(BF16)
        dkl_ref[:, cols(h)] = dot(probes, q_ref[:, cols(h)], 0, 0)
    stores[1].start()

    for copy in back1:
        copy.wait_recv()
    acc = jnp.zeros((PIECE, HEAD_DIM), F32)
    keep = jnp.ones((1, HEAD_DIM), F32)
    for i in range(CUBE - 1, -1, -1):
        suf_ref[i] = acc
        keep_buf[i] = keep
        hold = 1.0 - flag_buf[i]
        acc = hin_ref[i] + hold * acc
        keep = keep * hold
    htot_ref[pl.ds(0, PIECE)] = acc

    def down(b):
        return remote(
            htot_ref, htotin_ref.at[g], b2s.at[b], b2r.at[b], {"ctx": lax.rem(g + GROUPS - b, GROUPS) * CUBE + p}
        )

    for b in range(1, GROUPS):
        @pl.when(g - b >= 0)
        def _():
            down(b).start()

    for copy in gain1:
        copy.wait_recv()
    total = gg_buf[0]
    for i in range(1, CUBE):
        total = total + gg_buf[i]
    gt_src[...] = total
    gt_buf[g] = total
    gain2 = [
        remote(gt_src, gt_buf.at[g], g2s.at[b], g2r.at[b], {"ctx": lax.rem(g + b, GROUPS) * CUBE + p})
        for b in range(1, GROUPS)
    ]
    for copy in gain2:
        copy.start()

    for h in range(LOCAL):
        dvl_ref[:, cols(h)] = dot(w_ref[h], ga_ref[:, cols(h)], 0, 0)

    carry_ref[...] = jnp.zeros((PIECE, HEAD_DIM), F32)
    for b in range(GROUPS - 1, 0, -1):
        @pl.when(g + b < GROUPS)
        def _():
            down(b).wait_recv()
            at = lax.rem(g + b, GROUPS)
            hold = 1.0 - htotin_ref[at, pl.ds(PIECE, 1), :]
            carry_ref[...] = htotin_ref[at, pl.ds(0, PIECE), :] + hold * carry_ref[...]
    carry = carry_ref[...]
    back3 = []
    for a in range(1, CUBE):
        i = rank(a)
        rout_ref[i] = suf_ref[i] + keep_buf[i] * carry
        copy = remote(rout_ref.at[i], r_ref.at[p], b3s.at[a], b3r.at[a], {"ctx": base + i})
        copy.start()
        back3.append(copy)
    r_ref[p] = suf_ref[p] + keep_buf[p] * carry

    for copy in gain2:
        copy.wait_recv()
    dgain_ref[...] = (((gt_buf[0] + gt_buf[1]) + gt_buf[2]) + gt_buf[3]).reshape(LOCAL * HEAD_DIM)

    for copy in back3:
        copy.wait_recv()
    for h in range(LOCAL):
        upper, lower = halves(r_ref[pl.ds(4 * h, 4)].reshape(HEAD_DIM, HEAD_DIM))
        vt = vt_ref[:, cols(h)]
        kt = kt_ref[:, cols(h)]
        dk = dkl_ref[:, cols(h)] + dot(
            jnp.concatenate([vt, vt], axis=1), jnp.concatenate([upper, lower], axis=1), 1, 1
        )
        dk_ref[:, cols(h)] = dk.astype(BF16)
        dv = dvl_ref[:, cols(h)] + dot(
            jnp.concatenate([kt, kt], axis=1), jnp.concatenate([upper, lower], axis=0), 1, 0
        )
        dv_ref[:, cols(h)] = dv.astype(BF16)
    stores[2].start()
    stores[3].start()
    for copy in flags + level1 + level3 + shared + back1 + gain1 + gain2 + back3:
        copy.wait_send()
    for b in range(1, GROUPS):
        @pl.when(g + b < GROUPS)
        def _():
            up(b).wait_send()

        @pl.when(g - b >= 0)
        def _():
            down(b).wait_send()
    for store in stores:
        store.wait()


def per_device(queries, keys, values, d_out, gain, live_rows, doc_start):
    any_space = pl.BlockSpec(memory_space=pl.ANY)
    vmem = pl.BlockSpec(memory_space=pltpu.VMEM)
    wide = LOCAL * HEAD_DIM
    block = (ROWS, wide)
    pieces = (CUBE, PIECE, HEAD_DIM)
    dma = pltpu.SemaphoreType.DMA
    scratch = [pltpu.VMEM(block, BF16)] * 4
    scratch += [
        pltpu.VMEM((ROWS, ROWS), F32),
        pltpu.VMEM((LOCAL, ROWS, ROWS), BF16),
        pltpu.VMEM(block, F32),
        pltpu.VMEM(block, BF16),
        pltpu.VMEM(block, BF16),
        pltpu.VMEM(block, BF16),
        pltpu.VMEM((LOCAL, HEAD_DIM, ROWS), BF16),
        pltpu.VMEM(block, BF16),
        pltpu.VMEM(block, BF16),
    ]
    scratch += [pltpu.VMEM(block, BF16)] * 4 + [pltpu.VMEM(block, F32)] * 2
    scratch += [
        pltpu.VMEM((1, HEAD_DIM), F32),
        pltpu.VMEM((CUBE, 1, HEAD_DIM), F32),
        pltpu.VMEM((CUBE, 1, HEAD_DIM), F32),
    ]
    total = (PIECE + 8, HEAD_DIM)
    scratch += [
        pltpu.VMEM(pieces, F32),
        pltpu.VMEM(pieces, F32),
        pltpu.VMEM(pieces, F32),
        pltpu.VMEM(total, F32),
        pltpu.VMEM((GROUPS,) + total, F32),
        pltpu.VMEM((PIECE, HEAD_DIM), F32),
        pltpu.VMEM(pieces, F32),
        pltpu.VMEM(pieces, F32),
    ]
    scratch += [
        pltpu.VMEM(pieces, F32),
        pltpu.VMEM(pieces, F32),
        pltpu.VMEM(pieces, F32),
        pltpu.VMEM(total, F32),
        pltpu.VMEM((GROUPS,) + total, F32),
        pltpu.VMEM(pieces, F32),
        pltpu.VMEM(pieces, F32),
    ]
    scratch += [
        pltpu.VMEM((1, 2 * ROWS), F32),
        pltpu.VMEM((HEAD_PEERS, 1, 2 * ROWS), F32),
        pltpu.VMEM((1, wide), F32),
        pltpu.VMEM((CUBE, 1, wide), F32),
        pltpu.VMEM((1, wide), F32),
        pltpu.VMEM((GROUPS, 1, wide), F32),
    ]
    scratch += [dma((4,)), dma((4,))]
    for count in (CUBE, CUBE, GROUPS, CUBE, HEAD_PEERS, CUBE, GROUPS, CUBE, CUBE, GROUPS):
        scratch += [dma((count,)), dma((count,))]
    shape = jax.ShapeDtypeStruct(block, BF16)
    return pl.pallas_call(
        kernel,
        out_shape=(shape, shape, shape, shape, jax.ShapeDtypeStruct((wide,), F32)),
        in_specs=[any_space] * 4 + [vmem, pl.BlockSpec(memory_space=pltpu.SMEM), vmem],
        out_specs=(any_space,) * 4 + (vmem,),
        scratch_shapes=scratch,
        compiler_params=pltpu.CompilerParams(
            collective_id=0, has_side_effects=True, vmem_limit_bytes=40 * 1024 * 1024
        ),
    )(queries, keys, values, d_out, gain, live_rows, doc_start)


def solution(mesh):
    block = P("ctx", "head")
    return jax.shard_map(
        per_device,
        mesh=mesh,
        in_specs=(block, block, block, block, P("head"), P("ctx"), P("ctx")),
        out_specs=(block, block, block, block, P("head")),
        check_vma=False,
    )
```

```python
import jax
import jax.numpy as jnp
from jax import lax
from jax.experimental import pallas as pl
from jax.experimental.pallas import tpu as pltpu
from jax.sharding import PartitionSpec as P

HEADS = 32
HEAD_DIM = 128
D = HEADS * HEAD_DIM
EPSILON = 1e-06
ROWS = 256
LOCAL = 4
WIDE = LOCAL * HEAD_DIM
SIDE = 4
CUBE = 16
GROUPS = 4
PIECE = 32
PARTS = 2
SLAB = PIECE // PARTS
HEAD_PEERS = 8
MAIN_VMEM = 40 * 1024 * 1024
LAST_VMEM = 8 * 1024 * 1024
MESH = pl.DeviceIdType.MESH
F32 = jnp.float32
BF16 = jnp.bfloat16
OFFSETS = [(dz, dy) for dz in (2, 1, 3, 0) for dy in (2, 1, 3, 0) if (dz, dy) != (0, 0)]


def dot(a, b, ca, cb):
    return lax.dot_general(a, b, (((ca,), (cb,)), ((), ())), preferred_element_type=F32)


def halves(x):
    upper = x.astype(BF16)
    return upper, (x - upper.astype(F32)).astype(BF16)


def cols(h):
    return pl.ds(h * HEAD_DIM, HEAD_DIM)


def slab(part):
    return pl.ds(part * SLAB, SLAB)


def remote(src, dst, send, recv, where):
    return pltpu.make_async_remote_copy(
        src_ref=src, dst_ref=dst, send_sem=send, recv_sem=recv, device_id=where, device_id_type=MESH
    )


def main_kernel(
    q_hbm, k_hbm, v_hbm, y_hbm, gain_hbm, live_ref, doc_hbm,
    normed_ref, dq_ref, dkl_ref, dvl_ref, kt_ref, vt_ref, r_ref, dgain_ref,
    q_ref, k_ref, v_ref, y_ref, gain_ref, doc_ref,
    mask_ref, w_ref, att_ref, ga_ref, qh_ref, qht_ref,
    flag_src, flag_buf, keep_buf,
    t_ref, tin_ref, pre_ref, tot_ref, totin_ref, carry_ref, sout_ref, s_ref,
    h_ref, hin_ref, htot_ref, htotin_ref, rout_ref,
    ps_src, ps_buf, gg_src, gg_buf, gt_src, gt_buf,
    in_sem, ready, f_sem, ps_sem, gg_sem, gt_sem,
    l1s, l1r, l2s, l2r, l3s, l3r, b1s, b1r, b2s, b2r, b3s, b3r,
):
    c = lax.axis_index("ctx")
    me = lax.axis_index("head")
    p = lax.rem(c, CUBE)
    g = lax.div(c, CUBE)
    base = g * CUBE
    zl = lax.div(p, SIDE)
    yl = lax.rem(p, SIDE)
    ranks = [lax.rem(zl + dz, SIDE) * SIDE + lax.rem(yl + dy, SIDE) for dz, dy in OFFSETS]

    loads = [
        pltpu.make_async_copy(src, dst, in_sem.at[i])
        for i, (src, dst) in enumerate(
            (
                (k_hbm, k_ref), (v_hbm, v_ref), (doc_hbm, doc_ref),
                (q_hbm, q_ref), (y_hbm, y_ref), (gain_hbm, gain_ref),
            )
        )
    ]
    for load in loads:
        load.start()

    def above(b):
        return {"ctx": lax.rem(g + b, GROUPS) * CUBE + p}

    def below(b):
        return {"ctx": lax.rem(g + GROUPS - b, GROUPS) * CUBE + p}

    barrier = pltpu.get_barrier_semaphore()
    for b in range(1, GROUPS):
        @pl.when(g + b < GROUPS)
        def _():
            pl.semaphore_signal(barrier, inc=1, device_id=above(b), device_id_type=MESH)

    for i in ranks:
        pl.semaphore_signal(barrier, inc=1, device_id={"ctx": base + i}, device_id_type=MESH)
    for a in range(1, HEAD_PEERS):
        pl.semaphore_signal(
            barrier, inc=1, device_id={"head": lax.rem(me + a, HEAD_PEERS)}, device_id_type=MESH
        )

    loads[2].wait()
    live = live_ref[0]
    lane = lax.broadcasted_iota(jnp.int32, (ROWS, ROWS), 1)
    sub = lax.broadcasted_iota(jnp.int32, (ROWS, ROWS), 0)
    row8 = lax.broadcasted_iota(jnp.int32, (8, ROWS), 1)
    docs = jnp.broadcast_to(doc_ref[...].reshape(1, ROWS), (8, ROWS))
    starts = jnp.where(row8 < live, docs, 0).astype(F32).astype(BF16)
    upto = jnp.where(sub <= lane, 1.0, 0.0).astype(BF16)
    since = jnp.where(lane <= sub, 1.0, 0.0).astype(BF16)
    id_row = dot(starts, upto, 1, 0)[0:1, :]
    id_col = dot(since, starts, 1, 1)[:, 0:1]
    last = id_row[:, ROWS - 1 : ROWS]
    col = lax.broadcasted_iota(jnp.int32, (ROWS, 1), 0)
    live_col = jnp.where(col < live, 1.0, 0.0)
    tail_col = jnp.where(id_col == last, live_col, 0.0)
    head_col = jnp.where(id_col == 0.0, live_col, 0.0)
    flag = jnp.broadcast_to(jnp.where(last > 0.0, 1.0, 0.0), (1, HEAD_DIM))
    flag_src[...] = flag
    flag_buf[p] = flag
    tail_b = jnp.broadcast_to(tail_col, (ROWS, HEAD_DIM)).astype(BF16)
    head_b = jnp.broadcast_to(head_col, (ROWS, HEAD_DIM)).astype(BF16)
    live_b = jnp.broadcast_to(live_col, (ROWS, HEAD_DIM))

    loads[0].wait()
    loads[1].wait()
    for h in range(LOCAL):
        kt = k_ref[:, cols(h)] * tail_b
        kt_ref[:, cols(h)] = kt
        t_ref[pl.ds(4 * h, 4)] = dot(kt, v_ref[:, cols(h)], 0, 0).reshape(4, PIECE, HEAD_DIM)
    tin_ref[p] = t_ref[p]

    pl.semaphore_wait(barrier, CUBE - 1 + HEAD_PEERS - 1 + g)
    for b in range(1, GROUPS):
        @pl.when(g - b >= 0)
        def _():
            pl.semaphore_signal(ready.at[b], inc=1, device_id=below(b), device_id_type=MESH)

    flags = [remote(flag_src, flag_buf.at[p], f_sem.at[0], f_sem.at[1], {"ctx": base + i}) for i in ranks]
    for copy in flags:
        copy.start()

    def spread(src, dst, send, recv, part):
        for i in ranks:
            remote(
                src.at[i, slab(part)], dst.at[p, slab(part)], send.at[part], recv.at[part], {"ctx": base + i}
            ).start()

    def spread_all(ref, send, recv, part):
        whole = ref.at[pl.ds(0, CUBE - 1), slab(part)]
        return remote(whole, whole, send.at[part], recv.at[part], {"ctx": base + ranks[0]})

    def many(ref, count, sem, where):
        whole = ref.at[pl.ds(0, count)]
        return remote(whole, whole, sem.at[0], sem.at[1], where)

    near = {"ctx": base + ranks[0]}
    for part in range(PARTS):
        spread(t_ref, tin_ref, l1s, l1r, part)

    mask_ref[...] = jnp.where((id_col == id_row) & (lane <= sub), live_col, 0.0)
    loads[3].wait()
    for h in range(LOCAL):
        qs = q_ref[:, cols(h)]
        scores = dot(qs, k_ref[:, cols(h)], 1, 1)
        weights = (scores * mask_ref[...]).astype(BF16)
        w_ref[h] = weights
        att_ref[:, cols(h)] = dot(weights, v_ref[:, cols(h)], 1, 0)
        qh = qs * head_b
        qh_ref[:, cols(h)] = qh
        qht_ref[h] = qh.T
        vt_ref[:, cols(h)] = v_ref[:, cols(h)] * tail_b
    loads[4].wait()
    loads[5].wait()

    many(flag_buf, CUBE - 1, f_sem, near).wait_recv()
    keep = jnp.ones((1, HEAD_DIM), F32)
    for i in range(CUBE):
        keep_buf[i] = keep
        keep = keep * (1.0 - flag_buf[i])
    flag_tile = jnp.broadcast_to(1.0 - keep, (8, HEAD_DIM))
    tot_ref[pl.ds(0, 8)] = flag_tile
    htot_ref[pl.ds(0, 8)] = flag_tile

    def span(part):
        return pl.ds(0, 8 + SLAB) if part == 0 else pl.ds(8 + SLAB, SLAB)

    def rows_of(part):
        return pl.ds(8 + part * SLAB, SLAB)

    def up(b, part):
        return remote(
            tot_ref.at[span(part)], totin_ref.at[g, span(part)], l2s.at[part, b], l2r.at[part, b], above(b)
        )

    def down(b, part):
        return remote(
            htot_ref.at[span(part)], htotin_ref.at[g, span(part)], b2s.at[part, b], b2r.at[part, b], below(b)
        )

    def fold(order, source, partial, total, part):
        acc = jnp.zeros((SLAB, HEAD_DIM), F32)
        for i in order:
            partial[i, slab(part)] = acc
            acc = source[i, slab(part)] + (1.0 - flag_buf[i]) * acc
        total[rows_of(part)] = acc

    def finish(partial, out, into, send, recv, part):
        carry = carry_ref[slab(part)]
        for i in ranks:
            out[i, slab(part)] = partial[i, slab(part)] + keep_buf[i] * carry
            remote(
                out.at[i, slab(part)], into.at[p, slab(part)], send.at[part], recv.at[part], {"ctx": base + i}
            ).start()
        into[p, slab(part)] = partial[p, slab(part)] + keep_buf[p] * carry

    for part in range(PARTS):
        spread_all(tin_ref, l1s, l1r, part).wait_recv()
        fold(range(CUBE), tin_ref, pre_ref, tot_ref, part)
        for b in range(1, GROUPS):
            @pl.when(g + b < GROUPS)
            def _():
                if part == 0:
                    pl.semaphore_wait(ready.at[b], 1)
                up(b, part).start()

    for part in range(PARTS):
        carry_ref[slab(part)] = jnp.zeros((SLAB, HEAD_DIM), F32)
        for b in range(GROUPS - 1, 0, -1):
            @pl.when(g - b >= 0)
            def _():
                up(b, part).wait_recv()
                at = lax.rem(g + GROUPS - b, GROUPS)
                hold = 1.0 - totin_ref[at, pl.ds(0, 1), :]
                carry_ref[slab(part)] = totin_ref[at, rows_of(part), :] + hold * carry_ref[slab(part)]

        finish(pre_ref, sout_ref, s_ref, l3s, l3r, part)
    for part in range(PARTS):
        spread_all(s_ref, l3s, l3r, part).wait_recv()

    square = jnp.zeros((ROWS, HEAD_DIM), F32)
    inner = jnp.zeros((ROWS, HEAD_DIM), F32)
    for h in range(LOCAL):
        upper, lower = halves(s_ref[pl.ds(4 * h, 4)].reshape(HEAD_DIM, HEAD_DIM))
        qh = qh_ref[:, cols(h)]
        att = att_ref[:, cols(h)] + dot(
            jnp.concatenate([qh, qh], axis=1), jnp.concatenate([upper, lower], axis=0), 1, 0
        )
        att_ref[:, cols(h)] = att
        square = square + att * att
        gains = gain_ref[cols(h)].reshape(1, HEAD_DIM)
        inner = inner + att * (y_ref[:, cols(h)].astype(F32) * gains)
    ones = jnp.ones((8, 2 * HEAD_DIM), BF16)
    sums = [dot(ones, jnp.concatenate(halves(x), axis=1), 1, 1)[0:1, :] for x in (square, inner)]
    sums = jnp.concatenate(sums, axis=1)
    ps_src[...] = sums
    ps_buf[me] = sums
    for a in range(1, HEAD_PEERS):
        remote(
            ps_src, ps_buf.at[me], ps_sem.at[0], ps_sem.at[1], {"head": lax.rem(me + a, HEAD_PEERS)}
        ).start()
    side = {"head": lax.rem(me + 1, HEAD_PEERS)}
    many(ps_buf, HEAD_PEERS - 1, ps_sem, side).wait_recv()
    sums = ps_buf[0]
    for i in range(1, HEAD_PEERS):
        sums = sums + ps_buf[i]
    inverse = lax.rsqrt(sums[:, :ROWS] / D + EPSILON)
    factor = sums[:, ROWS:] * (inverse * inverse * inverse / D)
    inverse_col = jnp.broadcast_to(inverse, (HEAD_DIM, ROWS)).T
    factor_col = jnp.broadcast_to(factor, (HEAD_DIM, ROWS)).T

    for h in range(LOCAL):
        att = att_ref[:, cols(h)]
        y = y_ref[:, cols(h)].astype(F32)
        gains = gain_ref[cols(h)].reshape(1, HEAD_DIM)
        ga = ((y * gains) * inverse_col - att * factor_col) * live_b
        ga = ga.astype(BF16)
        ga_ref[:, cols(h)] = ga
        h_ref[pl.ds(4 * h, 4)] = dot(qht_ref[h], ga, 1, 0).reshape(4, PIECE, HEAD_DIM)
    hin_ref[p] = h_ref[p]
    for part in range(PARTS):
        spread(h_ref, hin_ref, b1s, b1r, part)

    gain_terms = []
    for h in range(LOCAL):
        att = att_ref[:, cols(h)]
        y = y_ref[:, cols(h)].astype(F32)
        gains = gain_ref[cols(h)].reshape(1, HEAD_DIM)
        unit = att * inverse_col
        normed_ref[:, cols(h)] = (unit * gains).astype(BF16)
        gain_terms.append(jnp.sum(y * unit, axis=0, keepdims=True))
    gain_term = jnp.concatenate(gain_terms, axis=1)
    gg_src[...] = gain_term
    gg_buf[p] = gain_term
    for i in ranks:
        remote(gg_src, gg_buf.at[p], gg_sem.at[0], gg_sem.at[1], {"ctx": base + i}).start()
    for h in range(LOCAL):
        ga = ga_ref[:, cols(h)]
        probes = (dot(ga, v_ref[:, cols(h)], 1, 1) * mask_ref[...]).astype(BF16)
        upper, lower = halves(s_ref[pl.ds(4 * h, 4)].reshape(HEAD_DIM, HEAD_DIM))
        gh = ga * head_b
        carried = dot(jnp.concatenate([gh, gh], axis=1), jnp.concatenate([upper, lower], axis=1), 1, 1)
        dq_ref[:, cols(h)] = (dot(probes, k_ref[:, cols(h)], 1, 0) + carried).astype(BF16)
        dkl_ref[:, cols(h)] = dot(probes, q_ref[:, cols(h)], 0, 0)
    keep = jnp.ones((1, HEAD_DIM), F32)
    for i in range(CUBE - 1, -1, -1):
        keep_buf[i] = keep
        keep = keep * (1.0 - flag_buf[i])

    for part in range(PARTS):
        spread_all(hin_ref, b1s, b1r, part).wait_recv()
        fold(range(CUBE - 1, -1, -1), hin_ref, pre_ref, htot_ref, part)
        for b in range(1, GROUPS):
            @pl.when(g - b >= 0)
            def _():
                down(b, part).start()

    many(gg_buf, CUBE - 1, gg_sem, near).wait_recv()
    total = gg_buf[0]
    for i in range(1, CUBE):
        total = total + gg_buf[i]
    gt_src[...] = total
    gt_buf[g] = total
    for b in range(1, GROUPS):
        remote(gt_src, gt_buf.at[g], gt_sem.at[0], gt_sem.at[1], above(b)).start()

    for h in range(LOCAL):
        dvl_ref[:, cols(h)] = dot(w_ref[h], ga_ref[:, cols(h)], 0, 0)

    for part in range(PARTS):
        carry_ref[slab(part)] = jnp.zeros((SLAB, HEAD_DIM), F32)
        for b in range(GROUPS - 1, 0, -1):
            @pl.when(g + b < GROUPS)
            def _():
                down(b, part).wait_recv()
                at = lax.rem(g + b, GROUPS)
                hold = 1.0 - htotin_ref[at, pl.ds(0, 1), :]
                carry_ref[slab(part)] = htotin_ref[at, rows_of(part), :] + hold * carry_ref[slab(part)]

        finish(pre_ref, rout_ref, r_ref, b3s, b3r, part)

    many(gt_buf, GROUPS - 1, gt_sem, above(1)).wait_recv()
    dgain_ref[...] = (((gt_buf[0] + gt_buf[1]) + gt_buf[2]) + gt_buf[3]).reshape(WIDE)

    many(flag_buf, CUBE - 1, f_sem, near).wait_send()
    many(ps_buf, HEAD_PEERS - 1, ps_sem, side).wait_send()
    many(gg_buf, CUBE - 1, gg_sem, near).wait_send()
    many(gt_buf, GROUPS - 1, gt_sem, above(1)).wait_send()
    for part in range(PARTS):
        spread_all(t_ref, l1s, l1r, part).wait_send()
        spread_all(sout_ref, l3s, l3r, part).wait_send()
        spread_all(h_ref, b1s, b1r, part).wait_send()
        for b in range(1, GROUPS):
            @pl.when(g + b < GROUPS)
            def _():
                up(b, part).wait_send()

            @pl.when(g - b >= 0)
            def _():
                down(b, part).wait_send()
    for part in range(PARTS):
        spread_all(rout_ref, b3s, b3r, part).wait_send()
    for part in range(PARTS):
        spread_all(r_ref, b3s, b3r, part).wait_recv()


def last_kernel(
    normed_ref, dq_ref, dkl_ref, dvl_ref, kt_ref, vt_ref, r_ref, dgain_ref,
    normed_hbm, dq_hbm, dk_hbm, dv_hbm, dgain_hbm,
    dk_ref, dv_ref, sems,
):
    stores = [
        pltpu.make_async_copy(src, dst, sems.at[i])
        for i, (src, dst) in enumerate(
            ((normed_ref, normed_hbm), (dq_ref, dq_hbm), (dgain_ref, dgain_hbm))
        )
    ]
    for store in stores:
        store.start()
    for h in range(LOCAL):
        upper, lower = halves(r_ref[pl.ds(4 * h, 4)].reshape(HEAD_DIM, HEAD_DIM))
        vt = vt_ref[:, cols(h)]
        kt = kt_ref[:, cols(h)]
        dk = dkl_ref[:, cols(h)] + dot(
            jnp.concatenate([vt, vt], axis=1), jnp.concatenate([upper, lower], axis=1), 1, 1
        )
        dk_ref[:, cols(h)] = dk.astype(BF16)
        dv = dvl_ref[:, cols(h)] + dot(
            jnp.concatenate([kt, kt], axis=1), jnp.concatenate([upper, lower], axis=0), 1, 0
        )
        dv_ref[:, cols(h)] = dv.astype(BF16)
        for i, (src, dst) in enumerate(((dk_ref, dk_hbm), (dv_ref, dv_hbm))):
            store = pltpu.make_async_copy(src.at[:, cols(h)], dst.at[:, cols(h)], sems.at[3 + 2 * h + i])
            store.start()
            stores.append(store)
    for store in stores:
        store.wait()


def stay(x):
    return pltpu.with_memory_space_constraint(x, pltpu.HBM)


def per_device(queries, keys, values, d_out, gain, live_rows, doc_start):
    hbm = pl.BlockSpec(memory_space=pltpu.HBM)
    vmem = pl.BlockSpec(memory_space=pltpu.VMEM)
    block = (ROWS, WIDE)
    pieces = (CUBE, PIECE, HEAD_DIM)
    total = (PIECE + 8, HEAD_DIM)
    dma = pltpu.SemaphoreType.DMA
    scratch = [pltpu.VMEM(block, BF16)] * 4
    scratch += [pltpu.VMEM((WIDE,), F32), pltpu.VMEM((ROWS,), jnp.int32)]
    scratch += [
        pltpu.VMEM((ROWS, ROWS), F32),
        pltpu.VMEM((LOCAL, ROWS, ROWS), BF16),
        pltpu.VMEM(block, F32),
        pltpu.VMEM(block, BF16),
        pltpu.VMEM(block, BF16),
        pltpu.VMEM((LOCAL, HEAD_DIM, ROWS), BF16),
    ]
    scratch += [
        pltpu.VMEM((1, HEAD_DIM), F32),
        pltpu.VMEM((CUBE, 1, HEAD_DIM), F32),
        pltpu.VMEM((CUBE, 1, HEAD_DIM), F32),
    ]
    scratch += [pltpu.VMEM(pieces, F32)] * 3
    scratch += [
        pltpu.VMEM(total, F32),
        pltpu.VMEM((GROUPS,) + total, F32),
        pltpu.VMEM((PIECE, HEAD_DIM), F32),
    ]
    scratch += [pltpu.VMEM(pieces, F32)] * 4
    scratch += [pltpu.VMEM(total, F32), pltpu.VMEM((GROUPS,) + total, F32), pltpu.VMEM(pieces, F32)]
    scratch += [
        pltpu.VMEM((1, 2 * ROWS), F32),
        pltpu.VMEM((HEAD_PEERS, 1, 2 * ROWS), F32),
        pltpu.VMEM((1, WIDE), F32),
        pltpu.VMEM((CUBE, 1, WIDE), F32),
        pltpu.VMEM((1, WIDE), F32),
        pltpu.VMEM((GROUPS, 1, WIDE), F32),
    ]
    scratch += [dma((6,)), pltpu.SemaphoreType.REGULAR((GROUPS,))] + [dma((2,))] * 4
    one, pairs = dma((PARTS,)), dma((PARTS, GROUPS))
    scratch += [one, one, pairs, pairs, one, one] * 2
    shape = jax.ShapeDtypeStruct(block, BF16)
    wide = jax.ShapeDtypeStruct(block, F32)
    gains = jax.ShapeDtypeStruct((WIDE,), F32)
    made = pl.pallas_call(
        main_kernel,
        out_shape=(shape, shape, wide, wide, shape, shape, jax.ShapeDtypeStruct(pieces, F32), gains),
        in_specs=[hbm] * 5 + [pl.BlockSpec(memory_space=pltpu.SMEM), hbm],
        out_specs=(vmem,) * 8,
        scratch_shapes=scratch,
        compiler_params=pltpu.CompilerParams(
            collective_id=0, has_side_effects=True, vmem_limit_bytes=MAIN_VMEM
        ),
    )(*(stay(x) for x in (queries, keys, values, d_out, gain)), live_rows, stay(doc_start))
    return pl.pallas_call(
        last_kernel,
        out_shape=(shape, shape, shape, shape, gains),
        in_specs=[vmem] * 8,
        out_specs=(hbm,) * 5,
        scratch_shapes=[pltpu.VMEM(block, BF16)] * 2 + [dma((3 + 2 * LOCAL,))],
        compiler_params=pltpu.CompilerParams(vmem_limit_bytes=LAST_VMEM),
    )(*made)


def solution(mesh):
    block = P("ctx", "head")
    return jax.shard_map(
        per_device,
        mesh=mesh,
        in_specs=(block, block, block, block, P("head"), P("ctx"), P("ctx")),
        out_specs=(block, block, block, block, P("head")),
        check_vma=False,
    )
```

```python
import jax
import jax.numpy as jnp
from jax import lax
from jax.experimental import pallas as pl
from jax.experimental.pallas import tpu as pltpu
from jax.sharding import PartitionSpec as P

HEADS = 32
HEAD_DIM = 128
D = HEADS * HEAD_DIM
EPSILON = 1e-06
ROWS = 256
LOCAL = 4
WIDE = LOCAL * HEAD_DIM
SIDE = 4
CUBE = 16
GROUPS = 4
PARTS = 4
PER = LOCAL // PARTS
SHARE = CUBE // PER
SLAB = 8 * PER
HEAD_PEERS = 8
MAIN_VMEM = 40 * 1024 * 1024
LAST_VMEM = 8 * 1024 * 1024
MESH = pl.DeviceIdType.MESH
F32 = jnp.float32
BF16 = jnp.bfloat16
OFFSETS = [(dz, dy) for dz in (2, 1, 3, 0) for dy in (2, 1, 3, 0) if (dz, dy) != (0, 0)]


def dot(a, b, ca, cb):
    return lax.dot_general(a, b, (((ca,), (cb,)), ((), ())), preferred_element_type=F32)


def halves(x):
    upper = x.astype(BF16)
    return upper, (x - upper.astype(F32)).astype(BF16)


def cols(h):
    return pl.ds(h * HEAD_DIM, HEAD_DIM)


def part_of(h):
    return h // PER


def share(h):
    return pl.ds(h % PER * SHARE, SHARE)


def remote(src, dst, send, recv, where):
    return pltpu.make_async_remote_copy(
        src_ref=src, dst_ref=dst, send_sem=send, recv_sem=recv, device_id=where, device_id_type=MESH
    )


def main_kernel(
    q_hbm, k_hbm, v_hbm, y_hbm, gain_hbm, live_ref, doc_hbm,
    normed_ref, dq_ref, dk_ref, dv_ref, dgain_ref,
    q_ref, k_ref, v_ref, y_ref, gain_ref, doc_ref,
    mask_ref, w_ref, att_ref, scaled_ref, dkl_ref, dvl_ref, ga_ref, qh_ref, kt_ref, vt_ref, qht_ref,
    flag_src, flag_buf, keep_buf,
    t_ref, tin_ref, pre_ref, tot_ref, totin_ref, carry_ref, sout_ref, s_ref,
    h_ref, hin_ref, htot_ref, htotin_ref, rout_ref, r_ref,
    ps_src, ps_buf, gy_src, gy_buf, gg_src, gg_buf, gt_src, gt_buf,
    in_sem, ready, f_sem, ps_sem, gy_sem, gg_sem, gt_sem,
    l1s, l1r, l2s, l2r, l3s, l3r, b1s, b1r, b2s, b2r, b3s, b3r,
):
    c = lax.axis_index("ctx")
    me = lax.axis_index("head")
    p = lax.rem(c, CUBE)
    g = lax.div(c, CUBE)
    base = g * CUBE
    zl = lax.div(p, SIDE)
    yl = lax.rem(p, SIDE)
    ranks = [lax.rem(zl + dz, SIDE) * SIDE + lax.rem(yl + dy, SIDE) for dz, dy in OFFSETS]

    loads = [
        pltpu.make_async_copy(src, dst, in_sem.at[i])
        for i, (src, dst) in enumerate(
            (
                (k_hbm, k_ref), (v_hbm, v_ref), (doc_hbm, doc_ref),
                (q_hbm, q_ref), (y_hbm, y_ref), (gain_hbm, gain_ref),
            )
        )
    ]
    for load in loads:
        load.start()

    def above(b):
        return {"ctx": lax.rem(g + b, GROUPS) * CUBE + p}

    def below(b):
        return {"ctx": lax.rem(g + GROUPS - b, GROUPS) * CUBE + p}

    def along_y(a):
        return {"ctx": base + zl * SIDE + lax.rem(yl + a, SIDE)}

    def along_z(a):
        return {"ctx": base + lax.rem(zl + a, SIDE) * SIDE + yl}

    barrier = pltpu.get_barrier_semaphore()
    for b in range(1, GROUPS):
        @pl.when(g + b < GROUPS)
        def _():
            pl.semaphore_signal(barrier, inc=1, device_id=above(b), device_id_type=MESH)

    for i in ranks:
        pl.semaphore_signal(barrier, inc=1, device_id={"ctx": base + i}, device_id_type=MESH)
    for a in range(1, HEAD_PEERS):
        pl.semaphore_signal(
            barrier, inc=1, device_id={"head": lax.rem(me + a, HEAD_PEERS)}, device_id_type=MESH
        )

    loads[2].wait()
    live = live_ref[0]
    lane1 = lax.broadcasted_iota(jnp.int32, (1, ROWS), 1)
    starts = (doc_ref[...].reshape(1, ROWS) > 0) & (lane1 < live)
    place = lane1.astype(F32)
    final = jnp.max(jnp.where(starts, place, -1.0), axis=1, keepdims=True)
    first = jnp.min(jnp.where(starts, place, float(ROWS)), axis=1, keepdims=True)
    col = lax.broadcasted_iota(jnp.int32, (ROWS, HEAD_DIM), 0)
    live_b = jnp.where(col < live, 1.0, 0.0)
    place_b = col.astype(F32)
    tail_b = jnp.where(place_b >= final, live_b, 0.0).astype(BF16)
    head_b = jnp.where(place_b < first, live_b, 0.0).astype(BF16)
    flag = jnp.broadcast_to(jnp.where(final >= 0.0, 1.0, 0.0), (1, HEAD_DIM))
    flag_src[...] = flag
    flag_buf[p] = flag

    loads[0].wait()
    loads[1].wait()
    for h in range(LOCAL):
        kt = k_ref[:, cols(h)] * tail_b
        kt_ref[:, cols(h)] = kt
        t_ref[part_of(h), share(h)] = dot(kt, v_ref[:, cols(h)], 0, 0).reshape(SHARE, SLAB, HEAD_DIM)
    for s in range(PARTS):
        tin_ref[s, p] = t_ref[s, p]

    pl.semaphore_wait(barrier, CUBE - 1 + HEAD_PEERS - 1 + g)
    for b in range(1, GROUPS):
        @pl.when(g - b >= 0)
        def _():
            pl.semaphore_signal(ready.at[b], inc=1, device_id=below(b), device_id_type=MESH)

    flags = [remote(flag_src, flag_buf.at[p], f_sem.at[0], f_sem.at[1], {"ctx": base + i}) for i in ranks]
    for copy in flags:
        copy.start()

    def spread(src, dst, send, recv, h):
        for i in ranks:
            remote(src.at[h, i], dst.at[h, p], send.at[h], recv.at[h], {"ctx": base + i}).start()

    def spread_all(ref, send, recv, h):
        whole = ref.at[h, pl.ds(0, CUBE - 1)]
        return remote(whole, whole, send.at[h], recv.at[h], {"ctx": base + ranks[0]})

    def many(ref, count, sem, where):
        whole = ref.at[pl.ds(0, count)]
        return remote(whole, whole, sem.at[0], sem.at[1], where)

    near = {"ctx": base + ranks[0]}
    for s in range(PARTS):
        spread(t_ref, tin_ref, l1s, l1r, s)

    lane = lax.broadcasted_iota(jnp.int32, (ROWS, ROWS), 1)
    sub = lax.broadcasted_iota(jnp.int32, (ROWS, ROWS), 0)
    upto = jnp.where(sub <= lane, 1.0, 0.0).astype(BF16)
    since = jnp.where(lane <= sub, 1.0, 0.0).astype(BF16)
    starts8 = jnp.broadcast_to(jnp.where(starts, 1.0, 0.0), (8, ROWS)).astype(BF16)
    id_row = dot(starts8, upto, 1, 0)[0:1, :]
    id_col = dot(since, starts8, 1, 1)[:, 0:1]
    live_col = live_b[:, 0:1]
    mask_ref[...] = jnp.where((id_col == id_row) & (lane <= sub), live_col, 0.0)
    loads[3].wait()
    for h in range(LOCAL):
        qs = q_ref[:, cols(h)]
        scores = dot(qs, k_ref[:, cols(h)], 1, 1)
        weights = (scores * mask_ref[...]).astype(BF16)
        w_ref[h] = weights
        att_ref[:, cols(h)] = dot(weights, v_ref[:, cols(h)], 1, 0)
        qh = qs * head_b
        qh_ref[:, cols(h)] = qh
        qht_ref[h] = qh.T
        vt_ref[:, cols(h)] = v_ref[:, cols(h)] * tail_b
    loads[4].wait()
    loads[5].wait()
    for h in range(LOCAL):
        scaled_ref[:, cols(h)] = y_ref[:, cols(h)].astype(F32) * gain_ref[cols(h)].reshape(1, HEAD_DIM)

    many(flag_buf, CUBE - 1, f_sem, near).wait_recv()
    keep = jnp.ones((1, HEAD_DIM), F32)
    for i in range(CUBE):
        keep_buf[i] = keep
        keep = keep * (1.0 - flag_buf[i])
    flag_tile = jnp.broadcast_to(1.0 - keep, (8, HEAD_DIM))
    tot_ref[pl.ds(0, 8)] = flag_tile
    htot_ref[pl.ds(0, 8)] = flag_tile

    def span(s):
        return pl.ds(0, 8 + SLAB) if s == 0 else rows_of(s)

    def rows_of(s):
        return pl.ds(8 + s * SLAB, SLAB)

    def up(b, s):
        return remote(tot_ref.at[span(s)], totin_ref.at[g, span(s)], l2s.at[s, b], l2r.at[s, b], above(b))

    def down(b, s):
        return remote(htot_ref.at[span(s)], htotin_ref.at[g, span(s)], b2s.at[s, b], b2r.at[s, b], below(b))

    def fold(order, source, partial, total, s):
        acc = jnp.zeros((SLAB, HEAD_DIM), F32)
        for i in order:
            partial[s, i] = acc
            acc = source[s, i] + (1.0 - flag_buf[i]) * acc
        total[rows_of(s)] = acc

    def finish(partial, out, into, send, recv, s):
        carry = carry_ref[s]
        for i in ranks:
            out[s, i] = partial[s, i] + keep_buf[i] * carry
            remote(out.at[s, i], into.at[s, p], send.at[s], recv.at[s], {"ctx": base + i}).start()
        into[s, p] = partial[s, p] + keep_buf[p] * carry

    for s in range(PARTS):
        spread_all(tin_ref, l1s, l1r, s).wait_recv()
        fold(range(CUBE), tin_ref, pre_ref, tot_ref, s)
        for b in range(1, GROUPS):
            @pl.when(g + b < GROUPS)
            def _():
                if s == 0:
                    pl.semaphore_wait(ready.at[b], 1)
                up(b, s).start()

    for s in range(PARTS):
        carry_ref[s] = jnp.zeros((SLAB, HEAD_DIM), F32)
        for b in range(GROUPS - 1, 0, -1):
            @pl.when(g - b >= 0)
            def _():
                up(b, s).wait_recv()
                at = lax.rem(g + GROUPS - b, GROUPS)
                hold = 1.0 - totin_ref[at, pl.ds(0, 1), :]
                carry_ref[s] = totin_ref[at, rows_of(s), :] + hold * carry_ref[s]

        finish(pre_ref, sout_ref, s_ref, l3s, l3r, s)

    square = jnp.zeros((ROWS, HEAD_DIM), F32)
    inner = jnp.zeros((ROWS, HEAD_DIM), F32)
    for h in range(LOCAL):
        if h % PER == 0:
            spread_all(s_ref, l3s, l3r, part_of(h)).wait_recv()
        upper, lower = halves(s_ref[part_of(h), share(h)].reshape(HEAD_DIM, HEAD_DIM))
        qh = qh_ref[:, cols(h)]
        att = att_ref[:, cols(h)] + dot(
            jnp.concatenate([qh, qh], axis=1), jnp.concatenate([upper, lower], axis=0), 1, 0
        )
        att_ref[:, cols(h)] = att
        square = square + att * att
        inner = inner + att * scaled_ref[:, cols(h)]
    ones = jnp.ones((8, 2 * HEAD_DIM), BF16)
    sums = [dot(ones, jnp.concatenate(halves(x), axis=1), 1, 1)[0:1, :] for x in (square, inner)]
    sums = jnp.concatenate(sums, axis=1)
    ps_src[...] = sums
    ps_buf[me] = sums
    for a in range(1, HEAD_PEERS):
        remote(
            ps_src, ps_buf.at[me], ps_sem.at[0], ps_sem.at[1], {"head": lax.rem(me + a, HEAD_PEERS)}
        ).start()
    side = {"head": lax.rem(me + 1, HEAD_PEERS)}
    many(ps_buf, HEAD_PEERS - 1, ps_sem, side).wait_recv()
    sums = ps_buf[0]
    for i in range(1, HEAD_PEERS):
        sums = sums + ps_buf[i]
    inverse = lax.rsqrt(sums[:, :ROWS] / D + EPSILON)
    factor = sums[:, ROWS:] * (inverse * inverse * inverse / D)
    alive = jnp.where(lane1 < live, 1.0, 0.0)
    inverse_col = jnp.broadcast_to(inverse * alive, (HEAD_DIM, ROWS)).T
    factor_col = jnp.broadcast_to(factor * alive, (HEAD_DIM, ROWS)).T

    for h in range(LOCAL):
        ga = (scaled_ref[:, cols(h)] * inverse_col - att_ref[:, cols(h)] * factor_col).astype(BF16)
        ga_ref[:, cols(h)] = ga
        h_ref[part_of(h), share(h)] = dot(qht_ref[h], ga, 1, 0).reshape(SHARE, SLAB, HEAD_DIM)
        if h % PER == PER - 1:
            hin_ref[part_of(h), p] = h_ref[part_of(h), p]
            spread(h_ref, hin_ref, b1s, b1r, part_of(h))

    gain_terms = []
    for h in range(LOCAL):
        att = att_ref[:, cols(h)]
        y = y_ref[:, cols(h)].astype(F32)
        gains = gain_ref[cols(h)].reshape(1, HEAD_DIM)
        unit = att * inverse_col
        normed_ref[:, cols(h)] = (unit * gains).astype(BF16)
        gain_terms.append(jnp.sum(y * unit, axis=0, keepdims=True))
    gain_term = jnp.concatenate(gain_terms, axis=1)
    gy_src[...] = gain_term
    gy_buf[yl] = gain_term
    for a in range(1, SIDE):
        remote(gy_src, gy_buf.at[yl], gy_sem.at[0], gy_sem.at[1], along_y(a)).start()
    for h in range(LOCAL):
        ga = ga_ref[:, cols(h)]
        probes = (dot(ga, v_ref[:, cols(h)], 1, 1) * mask_ref[...]).astype(BF16)
        upper, lower = halves(s_ref[part_of(h), share(h)].reshape(HEAD_DIM, HEAD_DIM))
        gh = ga * head_b
        carried = dot(jnp.concatenate([gh, gh], axis=1), jnp.concatenate([upper, lower], axis=1), 1, 1)
        dq_ref[:, cols(h)] = (dot(probes, k_ref[:, cols(h)], 1, 0) + carried).astype(BF16)
        dkl_ref[:, cols(h)] = dot(probes, q_ref[:, cols(h)], 0, 0)
    keep = jnp.ones((1, HEAD_DIM), F32)
    for i in range(CUBE - 1, -1, -1):
        keep_buf[i] = keep
        keep = keep * (1.0 - flag_buf[i])

    many(gy_buf, SIDE - 1, gy_sem, along_y(1)).wait_recv()
    total = ((gy_buf[0] + gy_buf[1]) + gy_buf[2]) + gy_buf[3]
    gg_src[...] = total
    gg_buf[zl] = total
    for a in range(1, SIDE):
        remote(gg_src, gg_buf.at[zl], gg_sem.at[0], gg_sem.at[1], along_z(a)).start()

    for s in range(PARTS):
        spread_all(hin_ref, b1s, b1r, s).wait_recv()
        fold(range(CUBE - 1, -1, -1), hin_ref, pre_ref, htot_ref, s)
        for b in range(1, GROUPS):
            @pl.when(g - b >= 0)
            def _():
                down(b, s).start()

    many(gg_buf, SIDE - 1, gg_sem, along_z(1)).wait_recv()
    total = ((gg_buf[0] + gg_buf[1]) + gg_buf[2]) + gg_buf[3]
    gt_src[...] = total
    gt_buf[g] = total
    for b in range(1, GROUPS):
        remote(gt_src, gt_buf.at[g], gt_sem.at[0], gt_sem.at[1], above(b)).start()

    for h in range(LOCAL):
        dvl_ref[:, cols(h)] = dot(w_ref[h], ga_ref[:, cols(h)], 0, 0)

    for s in range(PARTS):
        carry_ref[s] = jnp.zeros((SLAB, HEAD_DIM), F32)
        for b in range(GROUPS - 1, 0, -1):
            @pl.when(g + b < GROUPS)
            def _():
                down(b, s).wait_recv()
                at = lax.rem(g + b, GROUPS)
                hold = 1.0 - htotin_ref[at, pl.ds(0, 1), :]
                carry_ref[s] = htotin_ref[at, rows_of(s), :] + hold * carry_ref[s]

        finish(pre_ref, rout_ref, r_ref, b3s, b3r, s)

    many(gt_buf, GROUPS - 1, gt_sem, above(1)).wait_recv()
    dgain_ref[...] = (((gt_buf[0] + gt_buf[1]) + gt_buf[2]) + gt_buf[3]).reshape(WIDE)

    many(flag_buf, CUBE - 1, f_sem, near).wait_send()
    many(ps_buf, HEAD_PEERS - 1, ps_sem, side).wait_send()
    many(gy_buf, SIDE - 1, gy_sem, along_y(1)).wait_send()
    many(gg_buf, SIDE - 1, gg_sem, along_z(1)).wait_send()
    many(gt_buf, GROUPS - 1, gt_sem, above(1)).wait_send()
    for s in range(PARTS):
        spread_all(t_ref, l1s, l1r, s).wait_send()
        spread_all(sout_ref, l3s, l3r, s).wait_send()
        spread_all(h_ref, b1s, b1r, s).wait_send()
        for b in range(1, GROUPS):
            @pl.when(g + b < GROUPS)
            def _():
                up(b, s).wait_send()

            @pl.when(g - b >= 0)
            def _():
                down(b, s).wait_send()

    for h in range(LOCAL):
        if h % PER == 0:
            spread_all(r_ref, b3s, b3r, part_of(h)).wait_recv()
        upper, lower = halves(r_ref[part_of(h), share(h)].reshape(HEAD_DIM, HEAD_DIM))
        vt = vt_ref[:, cols(h)]
        kt = kt_ref[:, cols(h)]
        dk = dkl_ref[:, cols(h)] + dot(
            jnp.concatenate([vt, vt], axis=1), jnp.concatenate([upper, lower], axis=1), 1, 1
        )
        dk_ref[:, cols(h)] = dk.astype(BF16)
        dv = dvl_ref[:, cols(h)] + dot(
            jnp.concatenate([kt, kt], axis=1), jnp.concatenate([upper, lower], axis=0), 1, 0
        )
        dv_ref[:, cols(h)] = dv.astype(BF16)
    for s in range(PARTS):
        spread_all(rout_ref, b3s, b3r, s).wait_send()


def last_kernel(*refs):
    sems = refs[10]
    stores = [pltpu.make_async_copy(refs[i], refs[5 + i], sems.at[i]) for i in range(5)]
    for store in stores:
        store.start()
    for store in stores:
        store.wait()


def stay(x):
    return pltpu.with_memory_space_constraint(x, pltpu.HBM)


def per_device(queries, keys, values, d_out, gain, live_rows, doc_start):
    hbm = pl.BlockSpec(memory_space=pltpu.HBM)
    vmem = pl.BlockSpec(memory_space=pltpu.VMEM)
    block = (ROWS, WIDE)
    pieces = (PARTS, CUBE, SLAB, HEAD_DIM)
    total = (8 + PARTS * SLAB, HEAD_DIM)
    dma = pltpu.SemaphoreType.DMA
    scratch = [pltpu.VMEM(block, BF16)] * 4
    scratch += [pltpu.VMEM((WIDE,), F32), pltpu.VMEM((ROWS,), jnp.int32)]
    scratch += [
        pltpu.VMEM((ROWS, ROWS), F32),
        pltpu.VMEM((LOCAL, ROWS, ROWS), BF16),
    ]
    scratch += [pltpu.VMEM(block, F32)] * 4 + [pltpu.VMEM(block, BF16)] * 4
    scratch += [pltpu.VMEM((LOCAL, HEAD_DIM, ROWS), BF16)]
    scratch += [
        pltpu.VMEM((1, HEAD_DIM), F32),
        pltpu.VMEM((CUBE, 1, HEAD_DIM), F32),
        pltpu.VMEM((CUBE, 1, HEAD_DIM), F32),
    ]
    scratch += [pltpu.VMEM(pieces, F32)] * 3
    scratch += [
        pltpu.VMEM(total, F32),
        pltpu.VMEM((GROUPS,) + total, F32),
        pltpu.VMEM((PARTS, SLAB, HEAD_DIM), F32),
    ]
    scratch += [pltpu.VMEM(pieces, F32)] * 4
    scratch += [pltpu.VMEM(total, F32), pltpu.VMEM((GROUPS,) + total, F32)]
    scratch += [pltpu.VMEM(pieces, F32)] * 2
    scratch += [
        pltpu.VMEM((1, 2 * ROWS), F32),
        pltpu.VMEM((HEAD_PEERS, 1, 2 * ROWS), F32),
    ]
    scratch += [pltpu.VMEM((1, WIDE), F32), pltpu.VMEM((GROUPS, 1, WIDE), F32)] * 3
    scratch += [dma((6,)), pltpu.SemaphoreType.REGULAR((GROUPS,))] + [dma((2,))] * 5
    one, pairs = dma((PARTS,)), dma((PARTS, GROUPS))
    scratch += [one, one, pairs, pairs, one, one] * 2
    shape = jax.ShapeDtypeStruct(block, BF16)
    gains = jax.ShapeDtypeStruct((WIDE,), F32)
    made = pl.pallas_call(
        main_kernel,
        out_shape=(shape, shape, shape, shape, gains),
        in_specs=[hbm] * 5 + [pl.BlockSpec(memory_space=pltpu.SMEM), hbm],
        out_specs=(vmem,) * 5,
        scratch_shapes=scratch,
        compiler_params=pltpu.CompilerParams(
            collective_id=0, has_side_effects=True, vmem_limit_bytes=MAIN_VMEM
        ),
    )(*(stay(x) for x in (queries, keys, values, d_out, gain)), live_rows, stay(doc_start))
    return pl.pallas_call(
        last_kernel,
        out_shape=(shape, shape, shape, shape, gains),
        in_specs=[vmem] * 5,
        out_specs=(hbm,) * 5,
        scratch_shapes=[dma((5,))],
        compiler_params=pltpu.CompilerParams(vmem_limit_bytes=LAST_VMEM),
    )(*made)


def solution(mesh):
    block = P("ctx", "head")
    return jax.shard_map(
        per_device,
        mesh=mesh,
        in_specs=(block, block, block, block, P("head"), P("ctx"), P("ctx")),
        out_specs=(block, block, block, block, P("head")),
        check_vma=False,
    )
```

```python
import jax
import jax.numpy as jnp
from jax import lax
from jax.experimental import pallas as pl
from jax.experimental.pallas import tpu as pltpu
from jax.sharding import PartitionSpec as P

HEADS = 32
HEAD_DIM = 128
D = HEADS * HEAD_DIM
EPSILON = 1e-06
ROWS = 256
LOCAL = 4
WIDE = LOCAL * HEAD_DIM
SIDE = 4
CUBE = 16
GROUPS = 4
PARTS = 4
PER = LOCAL // PARTS
SHARE = CUBE // PER
SLAB = 8 * PER
HEAD_PEERS = 8
MAIN_VMEM = 40 * 1024 * 1024
LAST_VMEM = 8 * 1024 * 1024
MESH = pl.DeviceIdType.MESH
F32 = jnp.float32
BF16 = jnp.bfloat16
OFFSETS = [(dz, dy) for dy in (2, 1, 3, 0) for dz in (2, 1, 3, 0) if (dz, dy) != (0, 0)]


def dot(a, b, ca, cb):
    return lax.dot_general(a, b, (((ca,), (cb,)), ((), ())), preferred_element_type=F32)


def halves(x):
    upper = x.astype(BF16)
    return upper, (x - upper.astype(F32)).astype(BF16)


def cols(h):
    return pl.ds(h * HEAD_DIM, HEAD_DIM)


def part_of(h):
    return h // PER


def share(h):
    return pl.ds(h % PER * SHARE, SHARE)


def remote(src, dst, send, recv, where):
    return pltpu.make_async_remote_copy(
        src_ref=src, dst_ref=dst, send_sem=send, recv_sem=recv, device_id=where, device_id_type=MESH
    )


def main_kernel(
    q_hbm, k_hbm, v_hbm, y_hbm, gain_hbm, live_ref, doc_hbm,
    normed_ref, dq_ref, dk_ref, dv_ref, dgain_ref,
    q_ref, k_ref, v_ref, y_ref, gain_ref, doc_ref,
    mask_ref, w_ref, att_ref, scaled_ref, dkl_ref, dvl_ref, ga_ref, qh_ref, kt_ref, vt_ref, qht_ref,
    flag_src, flag_buf, keep_buf, fg_src, fg_buf,
    t_ref, tin_ref, pre_ref, tot_ref, totin_ref, carry_ref, sout_ref, s_ref,
    h_ref, hin_ref, htot_ref, htotin_ref, rout_ref, r_ref,
    ps_src, ps_buf, gy_src, gy_buf, gg_src, gg_buf, gt_src, gt_buf,
    in_sem, ready, fus, fur, fds, fdr, f_sem, ps_sem, gy_sem, gg_sem, gt_sem,
    l1s, l1r, l2s, l2r, l3s, l3r, b1s, b1r, b2s, b2r, b3s, b3r,
):
    c = lax.axis_index("ctx")
    me = lax.axis_index("head")
    p = lax.rem(c, CUBE)
    g = lax.div(c, CUBE)
    base = g * CUBE
    zl = lax.div(p, SIDE)
    yl = lax.rem(p, SIDE)
    ranks = [lax.rem(zl + dz, SIDE) * SIDE + lax.rem(yl + dy, SIDE) for dz, dy in OFFSETS]

    loads = [
        pltpu.make_async_copy(src, dst, in_sem.at[i])
        for i, (src, dst) in enumerate(
            (
                (k_hbm, k_ref), (v_hbm, v_ref), (doc_hbm, doc_ref),
                (q_hbm, q_ref), (y_hbm, y_ref), (gain_hbm, gain_ref),
            )
        )
    ]
    for load in loads:
        load.start()

    def above(b):
        return {"ctx": lax.rem(g + b, GROUPS) * CUBE + p}

    def below(b):
        return {"ctx": lax.rem(g + GROUPS - b, GROUPS) * CUBE + p}

    def along_y(a):
        return {"ctx": base + zl * SIDE + lax.rem(yl + a, SIDE)}

    def along_z(a):
        return {"ctx": base + lax.rem(zl + a, SIDE) * SIDE + yl}

    barrier = pltpu.get_barrier_semaphore()
    for b in range(1, GROUPS):
        @pl.when(g + b < GROUPS)
        def _():
            pl.semaphore_signal(barrier, inc=1, device_id=above(b), device_id_type=MESH)

    for i in ranks:
        pl.semaphore_signal(barrier, inc=1, device_id={"ctx": base + i}, device_id_type=MESH)
    for a in range(1, HEAD_PEERS):
        pl.semaphore_signal(
            barrier, inc=1, device_id={"head": lax.rem(me + a, HEAD_PEERS)}, device_id_type=MESH
        )

    loads[2].wait()
    live = live_ref[0]
    lane1 = lax.broadcasted_iota(jnp.int32, (1, ROWS), 1)
    starts = (doc_ref[...].reshape(1, ROWS) > 0) & (lane1 < live)
    place = lane1.astype(F32)
    final = jnp.max(jnp.where(starts, place, -1.0), axis=1, keepdims=True)
    first = jnp.min(jnp.where(starts, place, float(ROWS)), axis=1, keepdims=True)
    col = lax.broadcasted_iota(jnp.int32, (ROWS, HEAD_DIM), 0)
    live_b = jnp.where(col < live, 1.0, 0.0)
    place_b = col.astype(F32)
    tail_b = jnp.where(place_b >= final, live_b, 0.0).astype(BF16)
    head_b = jnp.where(place_b < first, live_b, 0.0).astype(BF16)
    flag = jnp.broadcast_to(jnp.where(final >= 0.0, 1.0, 0.0), (1, HEAD_DIM))
    flag_src[...] = flag
    flag_buf[p] = flag

    pl.semaphore_wait(barrier, CUBE - 1 + HEAD_PEERS - 1 + g)
    for b in range(1, GROUPS):
        @pl.when(g - b >= 0)
        def _():
            pl.semaphore_signal(ready.at[b], inc=1, device_id=below(b), device_id_type=MESH)

    flags = [remote(flag_src, flag_buf.at[p], f_sem.at[0], f_sem.at[1], {"ctx": base + i}) for i in ranks]
    for copy in flags:
        copy.start()

    def spread(src, dst, send, recv, h):
        for i in ranks:
            remote(src.at[h, i], dst.at[h, p], send.at[h], recv.at[h], {"ctx": base + i}).start()

    def spread_all(ref, send, recv, h):
        whole = ref.at[h, pl.ds(0, CUBE - 1)]
        return remote(whole, whole, send.at[h], recv.at[h], {"ctx": base + ranks[0]})

    def many(ref, count, sem, where):
        whole = ref.at[pl.ds(0, count)]
        return remote(whole, whole, sem.at[0], sem.at[1], where)

    near = {"ctx": base + ranks[0]}
    loads[0].wait()
    loads[1].wait()
    for h in range(LOCAL):
        kt = k_ref[:, cols(h)] * tail_b
        kt_ref[:, cols(h)] = kt
        t_ref[part_of(h), share(h)] = dot(kt, v_ref[:, cols(h)], 0, 0).reshape(SHARE, SLAB, HEAD_DIM)
        if h % PER == PER - 1:
            tin_ref[part_of(h), p] = t_ref[part_of(h), p]
            spread(t_ref, tin_ref, l1s, l1r, part_of(h))

    lane = lax.broadcasted_iota(jnp.int32, (ROWS, ROWS), 1)
    sub = lax.broadcasted_iota(jnp.int32, (ROWS, ROWS), 0)
    upto = jnp.where(sub <= lane, 1.0, 0.0).astype(BF16)
    since = jnp.where(lane <= sub, 1.0, 0.0).astype(BF16)
    starts8 = jnp.broadcast_to(jnp.where(starts, 1.0, 0.0), (8, ROWS)).astype(BF16)
    id_row = dot(starts8, upto, 1, 0)[0:1, :]
    id_col = dot(since, starts8, 1, 1)[:, 0:1]
    live_col = live_b[:, 0:1]
    mask_ref[...] = jnp.where((id_col == id_row) & (lane <= sub), live_col, 0.0)
    loads[3].wait()
    for h in range(LOCAL):
        qs = q_ref[:, cols(h)]
        scores = dot(qs, k_ref[:, cols(h)], 1, 1)
        weights = (scores * mask_ref[...]).astype(BF16)
        w_ref[h] = weights
        att_ref[:, cols(h)] = dot(weights, v_ref[:, cols(h)], 1, 0)
        qh = qs * head_b
        qh_ref[:, cols(h)] = qh
        qht_ref[h] = qh.T
        vt_ref[:, cols(h)] = v_ref[:, cols(h)] * tail_b
    loads[4].wait()
    loads[5].wait()
    for h in range(LOCAL):
        scaled_ref[:, cols(h)] = y_ref[:, cols(h)].astype(F32) * gain_ref[cols(h)].reshape(1, HEAD_DIM)

    many(flag_buf, CUBE - 1, f_sem, near).wait_recv()
    keep = jnp.ones((1, HEAD_DIM), F32)
    for i in range(CUBE):
        keep_buf[i] = keep
        keep = keep * (1.0 - flag_buf[i])
    fg_src[...] = 1.0 - keep

    def rows_of(s):
        return pl.ds(s * SLAB, SLAB)

    def up(b, s):
        return remote(
            tot_ref.at[rows_of(s)], totin_ref.at[g, rows_of(s)], l2s.at[s, b], l2r.at[s, b], above(b)
        )

    def down(b, s):
        return remote(
            htot_ref.at[rows_of(s)], htotin_ref.at[g, rows_of(s)], b2s.at[s, b], b2r.at[s, b], below(b)
        )

    def up_flag(b):
        return remote(fg_src, fg_buf.at[g], fus.at[b], fur.at[b], above(b))

    def down_flag(b):
        return remote(fg_src, fg_buf.at[g], fds.at[b], fdr.at[b], below(b))

    for b in range(1, GROUPS):
        @pl.when(g - b >= 0)
        def _():
            down_flag(b).start()

    def fold(order, source, partial, total, s):
        acc = jnp.zeros((SLAB, HEAD_DIM), F32)
        for i in order:
            partial[s, i] = acc
            acc = source[s, i] + (1.0 - flag_buf[i]) * acc
        total[rows_of(s)] = acc

    def finish(partial, out, into, send, recv, s):
        carry = carry_ref[s]
        for i in ranks:
            out[s, i] = partial[s, i] + keep_buf[i] * carry
            remote(out.at[s, i], into.at[s, p], send.at[s], recv.at[s], {"ctx": base + i}).start()
        into[s, p] = partial[s, p] + keep_buf[p] * carry

    for s in range(PARTS):
        spread_all(tin_ref, l1s, l1r, s).wait_recv()
        fold(range(CUBE), tin_ref, pre_ref, tot_ref, s)
        for b in range(1, GROUPS):
            @pl.when(g + b < GROUPS)
            def _():
                if s == 0:
                    pl.semaphore_wait(ready.at[b], 1)
                    up_flag(b).start()
                up(b, s).start()

    for s in range(PARTS):
        carry_ref[s] = jnp.zeros((SLAB, HEAD_DIM), F32)
        for b in range(GROUPS - 1, 0, -1):
            @pl.when(g - b >= 0)
            def _():
                if s == 0:
                    up_flag(b).wait_recv()
                up(b, s).wait_recv()
                at = lax.rem(g + GROUPS - b, GROUPS)
                hold = 1.0 - fg_buf[at]
                carry_ref[s] = totin_ref[at, rows_of(s), :] + hold * carry_ref[s]

        finish(pre_ref, sout_ref, s_ref, l3s, l3r, s)

    square = jnp.zeros((ROWS, HEAD_DIM), F32)
    inner = jnp.zeros((ROWS, HEAD_DIM), F32)
    for h in range(LOCAL):
        if h % PER == 0:
            spread_all(s_ref, l3s, l3r, part_of(h)).wait_recv()
        upper, lower = halves(s_ref[part_of(h), share(h)].reshape(HEAD_DIM, HEAD_DIM))
        qh = qh_ref[:, cols(h)]
        att = att_ref[:, cols(h)] + dot(
            jnp.concatenate([qh, qh], axis=1), jnp.concatenate([upper, lower], axis=0), 1, 0
        )
        att_ref[:, cols(h)] = att
        square = square + att * att
        inner = inner + att * scaled_ref[:, cols(h)]
    ones = jnp.ones((8, 2 * HEAD_DIM), BF16)
    sums = [dot(ones, jnp.concatenate(halves(x), axis=1), 1, 1)[0:1, :] for x in (square, inner)]
    sums = jnp.concatenate(sums, axis=1)
    ps_src[...] = sums
    ps_buf[me] = sums
    for a in range(1, HEAD_PEERS):
        remote(
            ps_src, ps_buf.at[me], ps_sem.at[0], ps_sem.at[1], {"head": lax.rem(me + a, HEAD_PEERS)}
        ).start()
    side = {"head": lax.rem(me + 1, HEAD_PEERS)}
    many(ps_buf, HEAD_PEERS - 1, ps_sem, side).wait_recv()
    sums = ps_buf[0]
    for i in range(1, HEAD_PEERS):
        sums = sums + ps_buf[i]
    inverse = lax.rsqrt(sums[:, :ROWS] / D + EPSILON)
    factor = sums[:, ROWS:] * (inverse * inverse * inverse / D)
    alive = jnp.where(lane1 < live, 1.0, 0.0)
    inverse_col = jnp.broadcast_to(inverse * alive, (HEAD_DIM, ROWS)).T
    factor_col = jnp.broadcast_to(factor * alive, (HEAD_DIM, ROWS)).T

    for h in range(LOCAL):
        ga = (scaled_ref[:, cols(h)] * inverse_col - att_ref[:, cols(h)] * factor_col).astype(BF16)
        ga_ref[:, cols(h)] = ga
        h_ref[part_of(h), share(h)] = dot(qht_ref[h], ga, 1, 0).reshape(SHARE, SLAB, HEAD_DIM)
        if h % PER == PER - 1:
            hin_ref[part_of(h), p] = h_ref[part_of(h), p]
            spread(h_ref, hin_ref, b1s, b1r, part_of(h))

    gain_terms = []
    for h in range(LOCAL):
        att = att_ref[:, cols(h)]
        y = y_ref[:, cols(h)].astype(F32)
        gains = gain_ref[cols(h)].reshape(1, HEAD_DIM)
        unit = att * inverse_col
        normed_ref[:, cols(h)] = (unit * gains).astype(BF16)
        gain_terms.append(jnp.sum(y * unit, axis=0, keepdims=True))
    gain_term = jnp.concatenate(gain_terms, axis=1)
    gy_src[...] = gain_term
    gy_buf[yl] = gain_term
    for a in range(1, SIDE):
        remote(gy_src, gy_buf.at[yl], gy_sem.at[0], gy_sem.at[1], along_y(a)).start()
    for h in range(LOCAL):
        ga = ga_ref[:, cols(h)]
        probes = (dot(ga, v_ref[:, cols(h)], 1, 1) * mask_ref[...]).astype(BF16)
        upper, lower = halves(s_ref[part_of(h), share(h)].reshape(HEAD_DIM, HEAD_DIM))
        gh = ga * head_b
        carried = dot(jnp.concatenate([gh, gh], axis=1), jnp.concatenate([upper, lower], axis=1), 1, 1)
        dq_ref[:, cols(h)] = (dot(probes, k_ref[:, cols(h)], 1, 0) + carried).astype(BF16)
        dkl_ref[:, cols(h)] = dot(probes, q_ref[:, cols(h)], 0, 0)
    keep = jnp.ones((1, HEAD_DIM), F32)
    for i in range(CUBE - 1, -1, -1):
        keep_buf[i] = keep
        keep = keep * (1.0 - flag_buf[i])

    many(gy_buf, SIDE - 1, gy_sem, along_y(1)).wait_recv()
    total = ((gy_buf[0] + gy_buf[1]) + gy_buf[2]) + gy_buf[3]
    gg_src[...] = total
    gg_buf[zl] = total
    for a in range(1, SIDE):
        remote(gg_src, gg_buf.at[zl], gg_sem.at[0], gg_sem.at[1], along_z(a)).start()

    for s in range(PARTS):
        spread_all(hin_ref, b1s, b1r, s).wait_recv()
        fold(range(CUBE - 1, -1, -1), hin_ref, pre_ref, htot_ref, s)
        for b in range(1, GROUPS):
            @pl.when(g - b >= 0)
            def _():
                down(b, s).start()

    many(gg_buf, SIDE - 1, gg_sem, along_z(1)).wait_recv()
    total = ((gg_buf[0] + gg_buf[1]) + gg_buf[2]) + gg_buf[3]
    gt_src[...] = total
    gt_buf[g] = total
    for b in range(1, GROUPS):
        remote(gt_src, gt_buf.at[g], gt_sem.at[0], gt_sem.at[1], above(b)).start()

    for h in range(LOCAL):
        dvl_ref[:, cols(h)] = dot(w_ref[h], ga_ref[:, cols(h)], 0, 0)

    for s in range(PARTS):
        carry_ref[s] = jnp.zeros((SLAB, HEAD_DIM), F32)
        for b in range(GROUPS - 1, 0, -1):
            @pl.when(g + b < GROUPS)
            def _():
                if s == 0:
                    down_flag(b).wait_recv()
                down(b, s).wait_recv()
                at = lax.rem(g + b, GROUPS)
                hold = 1.0 - fg_buf[at]
                carry_ref[s] = htotin_ref[at, rows_of(s), :] + hold * carry_ref[s]

        finish(pre_ref, rout_ref, r_ref, b3s, b3r, s)

    many(gt_buf, GROUPS - 1, gt_sem, above(1)).wait_recv()
    dgain_ref[...] = (((gt_buf[0] + gt_buf[1]) + gt_buf[2]) + gt_buf[3]).reshape(WIDE)

    many(flag_buf, CUBE - 1, f_sem, near).wait_send()
    many(ps_buf, HEAD_PEERS - 1, ps_sem, side).wait_send()
    many(gy_buf, SIDE - 1, gy_sem, along_y(1)).wait_send()
    many(gg_buf, SIDE - 1, gg_sem, along_z(1)).wait_send()
    many(gt_buf, GROUPS - 1, gt_sem, above(1)).wait_send()
    for s in range(PARTS):
        spread_all(t_ref, l1s, l1r, s).wait_send()
        spread_all(sout_ref, l3s, l3r, s).wait_send()
        spread_all(h_ref, b1s, b1r, s).wait_send()
        for b in range(1, GROUPS):
            @pl.when(g + b < GROUPS)
            def _():
                if s == 0:
                    up_flag(b).wait_send()
                up(b, s).wait_send()

            @pl.when(g - b >= 0)
            def _():
                if s == 0:
                    down_flag(b).wait_send()
                down(b, s).wait_send()

    for h in range(LOCAL):
        if h % PER == 0:
            spread_all(r_ref, b3s, b3r, part_of(h)).wait_recv()
        upper, lower = halves(r_ref[part_of(h), share(h)].reshape(HEAD_DIM, HEAD_DIM))
        vt = vt_ref[:, cols(h)]
        kt = kt_ref[:, cols(h)]
        dk = dkl_ref[:, cols(h)] + dot(
            jnp.concatenate([vt, vt], axis=1), jnp.concatenate([upper, lower], axis=1), 1, 1
        )
        dk_ref[:, cols(h)] = dk.astype(BF16)
        dv = dvl_ref[:, cols(h)] + dot(
            jnp.concatenate([kt, kt], axis=1), jnp.concatenate([upper, lower], axis=0), 1, 0
        )
        dv_ref[:, cols(h)] = dv.astype(BF16)
    for s in range(PARTS):
        spread_all(rout_ref, b3s, b3r, s).wait_send()


def last_kernel(*refs):
    sems = refs[10]
    stores = [pltpu.make_async_copy(refs[i], refs[5 + i], sems.at[i]) for i in range(5)]
    for store in stores:
        store.start()
    for store in stores:
        store.wait()


def stay(x):
    return pltpu.with_memory_space_constraint(x, pltpu.HBM)


def per_device(queries, keys, values, d_out, gain, live_rows, doc_start):
    hbm = pl.BlockSpec(memory_space=pltpu.HBM)
    vmem = pl.BlockSpec(memory_space=pltpu.VMEM)
    block = (ROWS, WIDE)
    pieces = (PARTS, CUBE, SLAB, HEAD_DIM)
    total = (PARTS * SLAB, HEAD_DIM)
    dma = pltpu.SemaphoreType.DMA
    scratch = [pltpu.VMEM(block, BF16)] * 4
    scratch += [pltpu.VMEM((WIDE,), F32), pltpu.VMEM((ROWS,), jnp.int32)]
    scratch += [
        pltpu.VMEM((ROWS, ROWS), F32),
        pltpu.VMEM((LOCAL, ROWS, ROWS), BF16),
    ]
    scratch += [pltpu.VMEM(block, F32)] * 4 + [pltpu.VMEM(block, BF16)] * 4
    scratch += [pltpu.VMEM((LOCAL, HEAD_DIM, ROWS), BF16)]
    scratch += [
        pltpu.VMEM((1, HEAD_DIM), F32),
        pltpu.VMEM((CUBE, 1, HEAD_DIM), F32),
        pltpu.VMEM((CUBE, 1, HEAD_DIM), F32),
        pltpu.VMEM((1, HEAD_DIM), F32),
        pltpu.VMEM((GROUPS, 1, HEAD_DIM), F32),
    ]
    scratch += [pltpu.VMEM(pieces, F32)] * 3
    scratch += [
        pltpu.VMEM(total, F32),
        pltpu.VMEM((GROUPS,) + total, F32),
        pltpu.VMEM((PARTS, SLAB, HEAD_DIM), F32),
    ]
    scratch += [pltpu.VMEM(pieces, F32)] * 4
    scratch += [pltpu.VMEM(total, F32), pltpu.VMEM((GROUPS,) + total, F32)]
    scratch += [pltpu.VMEM(pieces, F32)] * 2
    scratch += [
        pltpu.VMEM((1, 2 * ROWS), F32),
        pltpu.VMEM((HEAD_PEERS, 1, 2 * ROWS), F32),
    ]
    scratch += [pltpu.VMEM((1, WIDE), F32), pltpu.VMEM((GROUPS, 1, WIDE), F32)] * 3
    scratch += [dma((6,)), pltpu.SemaphoreType.REGULAR((GROUPS,))]
    scratch += [dma((GROUPS,))] * 4 + [dma((2,))] * 5
    one, pairs = dma((PARTS,)), dma((PARTS, GROUPS))
    scratch += [one, one, pairs, pairs, one, one] * 2
    shape = jax.ShapeDtypeStruct(block, BF16)
    gains = jax.ShapeDtypeStruct((WIDE,), F32)
    made = pl.pallas_call(
        main_kernel,
        out_shape=(shape, shape, shape, shape, gains),
        in_specs=[hbm] * 5 + [pl.BlockSpec(memory_space=pltpu.SMEM), hbm],
        out_specs=(vmem,) * 5,
        scratch_shapes=scratch,
        compiler_params=pltpu.CompilerParams(
            collective_id=0, has_side_effects=True, vmem_limit_bytes=MAIN_VMEM
        ),
    )(*(stay(x) for x in (queries, keys, values, d_out, gain)), live_rows, stay(doc_start))
    return pl.pallas_call(
        last_kernel,
        out_shape=(shape, shape, shape, shape, gains),
        in_specs=[vmem] * 5,
        out_specs=(hbm,) * 5,
        scratch_shapes=[dma((5,))],
        compiler_params=pltpu.CompilerParams(vmem_limit_bytes=LAST_VMEM),
    )(*made)


def solution(mesh):
    block = P("ctx", "head")
    return jax.shard_map(
        per_device,
        mesh=mesh,
        in_specs=(block, block, block, block, P("head"), P("ctx"), P("ctx")),
        out_specs=(block, block, block, block, P("head")),
        check_vma=False,
    )
```
